256 devices in a mesh: load: 16 (over x, z_hi), space: 16 (over y, z_lo, core).
Axes of the slice: x: 4, y: 4, z: 8 (z_hi: 4, z_lo: 2; z = z_hi * 2 + z_lo), core: 2. Of those that a mesh axis runs over, the one named last changes fastest.
Arguments:
- density: float32 [32, 32, 256], P('space', 'load'), may hold values from 0.3 to 1
- fixed_mask: int32 [32, 32, 256], P('space'), may hold values 0 or 1
- patch_index: int32 [32, 32, 256], P('space'), may hold values from 0 to 15
- patch_force: float32 [16, 3, 16], P('load'), may hold values from -6 to 6
Outputs:
- displacement: float32 [16, 3, 32, 32, 256], P('load', None, 'space')
- sensitivity: float32 [32, 32, 256], P('space', 'load')
The draws below stay inside these ranges and needn't reach their ends.
Inputs may be any that keep to these rules, and one draw needn't show every extreme that they name: `fixed_mask`: 1 marks a node held fixed.
All inputs are finite; a program needn't handle non-finite values. No bound on the sum of `fixed_mask` on one device may be relied on, other than what follows from the above.
Results may differ from the reference program's by a relative error of at most 0.00027.
Values sent between devices are 32-bit elements; how exact they have to be, the bound alone decides.
No kernel may reach another device: no remote copies, remote signals or barrier semaphores. Data moves between devices by JAX's collectives and lax.ppermute only.
A program may use at most 64 MiB of HBM per device.

```python
import math
import jax
import jax.numpy as jnp
import numpy as np
from jax import lax

NY = 32
NZ = 256
ITERS = 3
PATCHES = 16
LOADS = 16
NX = 32


def with_ends(values, stream_key, low, largest):
    shape = values.shape
    index_at = [jax.random.randint(jax.random.fold_in(stream_key, axis), (), 0, shape[axis]) for axis in range(len(shape))]
    values = values.at[tuple(index_at)].set(low)
    longest = shape.index(max(shape))
    index_at[longest] = (index_at[longest] + 1) % shape[longest]
    return values.at[tuple(index_at)].set(largest)


def block_levels(own_key, extent, cuts, least, largest):
    level = 1.0
    for dim, blocks in cuts:
        steps = jax.random.uniform(jax.random.fold_in(jax.random.fold_in(own_key, 6), dim), (blocks,), jnp.float32, least / len(cuts), largest / len(cuts))
        level = level * jnp.repeat(jnp.exp(steps), extent[dim] // blocks).reshape((-1,) + (1,) * (len(extent) - 1 - dim))
    return level


def normal_values(key, shape, deviation, reach, cuts=(), held_as=jnp.bfloat16):
    drawn = jax.random.normal(key, shape, jnp.float32) * deviation
    if len(cuts) > 0:
        drawn = block_levels(key, shape, cuts, -0.22, 0.18) * drawn
    return jnp.clip(drawn, min=-reach, max=reach).astype(held_as)


def setup_inputs(seed: int = 0) -> dict:
    key_list = jax.random.split(jax.random.key(seed), 5)
    density = jnp.clip(0.3 + 0.7 * jax.random.uniform(key_list[0], (NX, NY, NZ), jnp.float32) ** block_levels(key_list[0], (NX, NY, NZ), ((0, 16), (1, 16)), -0.2, 0.2), 0.3, 1.0)
    fixed_mask = with_ends((jax.random.randint(key_list[1], (NX, NY, NZ), 0, 8) < 1).astype(jnp.int32), jax.random.fold_in(key_list[1], 1), 0, 1)
    patch_index = with_ends(jax.random.randint(key_list[2], (NX, NY, NZ), 0, PATCHES), jax.random.fold_in(key_list[2], 1), 0, PATCHES - 1).astype(jnp.int32)
    patch_force = normal_values(key_list[3], (LOADS, 3, PATCHES), 1.0, 6.0, ((0, 16),), jnp.float32)
    return dict(density=density, fixed_mask=fixed_mask, patch_index=patch_index, patch_force=patch_force)


void_stiffness = 0.001
poisson_ratio = 0.3

def corner_offsets(corner):
    return (corner % 2, corner // 2 % 2, corner // 4)

def element_matrix():
    lame_first = poisson_ratio / ((1.0 + poisson_ratio) * (1.0 - 2.0 * poisson_ratio))
    shear_modulus = 0.5 / (1.0 + poisson_ratio)
    elastic = np.zeros((6, 6))
    elastic[:3, :3] = lame_first
    for diag_index in range(3):
        elastic[diag_index, diag_index] = lame_first + 2.0 * shear_modulus
        elastic[diag_index + 3, diag_index + 3] = shear_modulus
    points = [0.5 - 0.5 / math.sqrt(3.0), 0.5 + 0.5 / math.sqrt(3.0)]
    result = np.zeros((24, 24))
    for point_x in points:
        for point_y in points:
            for point_z in points:
                strain = np.zeros((6, 24))
                for corner in range(8):
                    offset_x, offset_y, offset_z = corner_offsets(corner)
                    shape_x = point_x if offset_x else 1.0 - point_x
                    shape_y = point_y if offset_y else 1.0 - point_y
                    shape_z = point_z if offset_z else 1.0 - point_z
                    slope_x = 1.0 if offset_x else -1.0
                    slope_y = 1.0 if offset_y else -1.0
                    slope_z = 1.0 if offset_z else -1.0
                    grad_x = slope_x * shape_y * shape_z
                    grad_y = shape_x * slope_y * shape_z
                    grad_z = shape_x * shape_y * slope_z
                    column = 3 * corner
                    strain[0, column] = grad_x
                    strain[1, column + 1] = grad_y
                    strain[2, column + 2] = grad_z
                    strain[3, column] = grad_y
                    strain[3, column + 1] = grad_x
                    strain[4, column + 1] = grad_z
                    strain[4, column + 2] = grad_y
                    strain[5, column] = grad_z
                    strain[5, column + 2] = grad_x
                result = result + strain.T @ elastic @ strain / 8.0
    return result

def corner_slice(padded, corner, layers):
    offset_x, offset_y, offset_z = corner_offsets(corner)
    across_rows = padded.shape[2] - 1
    depth_cols = padded.shape[3] - 1
    return padded[:, offset_x:offset_x + layers, offset_y:offset_y + across_rows, offset_z:offset_z + depth_cols]

def place_nodes(corner_term, corner, lead_layers, planes):
    offset_x, offset_y, offset_z = corner_offsets(corner)
    padded_term = jnp.pad(corner_term, ((0, 0), (1, 1), (1, 0), (1, 0)))
    start_plane = lead_layers + 1 - offset_x
    across_rows = corner_term.shape[2]
    depth_cols = corner_term.shape[3]
    return padded_term[:, start_plane:start_plane + planes, 1 - offset_y:1 - offset_y + across_rows, 1 - offset_z:1 - offset_z + depth_cols]

def diagonal_nodes(matrix, weights, lead_layers, planes):
    summed = None
    for target in range(8):
        entries = jnp.asarray([float(matrix[3 * target + component, 3 * target + component]) for component in range(3)], jnp.float32)
        placed = place_nodes(entries[:, None, None, None] * weights[None], target, lead_layers, planes)
        summed = placed if target == 0 else summed + placed
    return summed

def case_force(case_table, patch_index, span_ramp, free_mask):
    summed = jnp.zeros((3,) + patch_index.shape, jnp.float32)
    for region in range(case_table.shape[1]):
        summed = summed + jnp.where((patch_index == region)[None], case_table[:, region][:, None, None, None], 0.0)
    return summed * span_ramp[None, :, None, None] * free_mask[None]

def stacked_corners(padded, layers):
    pieces = []
    for corner in range(8):
        pieces.append(corner_slice(padded, corner, layers))
    return jnp.concatenate(pieces, 0)

def pad_all(vector_field):
    return jnp.pad(vector_field, ((0, 0), (0, 1), (0, 1), (0, 1)))

def reference(density, fixed_mask, patch_index, patch_force):
    matrix = element_matrix()
    matrix_table = jnp.asarray(matrix, jnp.float32)
    stiffness = void_stiffness + (1.0 - void_stiffness) * density ** 3
    free_mask = jnp.where(fixed_mask == 0, 1.0, 0.0).astype(jnp.float32)
    planes = density.shape[0]
    diagonal = diagonal_nodes(matrix, stiffness, 0, planes)
    precond = free_mask * diagonal + (1.0 - free_mask)
    span_ramp = 1.0 + 2.0 * jnp.arange(planes, dtype=jnp.float32) / (planes - 1)

    def element_values(vector_field):
        stacked = stacked_corners(pad_all(vector_field), planes)
        applied = jnp.einsum('ab,bxyz->axyz', matrix_table, stacked, precision=lax.Precision.HIGHEST)
        return (stacked, applied)

    def operate(vector_field):
        stacked, applied = element_values(vector_field)
        weighted = applied * stiffness[None]
        summed = None
        for target in range(8):
            placed = place_nodes(weighted[3 * target:3 * target + 3], target, 0, planes)
            summed = placed if target == 0 else summed + placed
        return free_mask * summed

    def solve_case(case_table):
        residual = case_force(case_table, patch_index, span_ramp, free_mask)
        precon_res = residual / precond
        direction = precon_res
        weighted_now = jnp.sum(residual * precon_res)
        solution = jnp.zeros_like(residual)
        for iteration in range(ITERS):
            applied = operate(direction)
            step_size = weighted_now / jnp.sum(direction * applied)
            solution = solution + step_size * direction
            if iteration + 1 < ITERS:
                residual = residual - step_size * applied
                precon_res = residual / precond
                weighted_next = jnp.sum(residual * precon_res)
                direction = precon_res + weighted_next / weighted_now * direction
                weighted_now = weighted_next
        stacked, applied = element_values(solution)
        energy = lax.optimization_barrier(jnp.sum(stacked * applied, axis=0))
        return (solution, energy)
    solutions, energies = lax.map(solve_case, patch_force)
    sensitivity = -3.0 * (1.0 - void_stiffness) * density ** 2 * lax.optimization_barrier(jnp.mean(energies, axis=0))
    return (solutions, sensitivity)
```

```python
import jax
import jax.numpy as jnp
from jax import lax
from jax.experimental import pallas as pl
from jax.experimental.pallas import tpu as pltpu
from jax.sharding import PartitionSpec as P

NX, NY, NZ = 32, 32, 256
PATCHES = 16
LOADS = 16
OUTSIDE = 16.0
void_stiffness = 0.001
poisson_ratio = 0.3
LAME = poisson_ratio / ((1.0 + poisson_ratio) * (1.0 - 2.0 * poisson_ratio))
SHEAR = 0.5 / (1.0 + poisson_ratio)
DIAGONAL = (LAME + 4.0 * SHEAR) / 9.0
MODE_SCALE = 1.0 / 16.0


def next_y(v, last):
    return jnp.where(last, 0.0, pltpu.roll(v, v.shape[0] - 1, 0))


def prev_y(v, first):
    return jnp.where(first, 0.0, pltpu.roll(v, 1, 0))


def next_z(v, last):
    return jnp.where(last, 0.0, pltpu.roll(v, v.shape[1] - 1, 1))


def prev_z(v, first):
    return jnp.where(first, 0.0, pltpu.roll(v, 1, 1))


def plane_edges():
    row = lax.broadcasted_iota(jnp.int32, (NY, NZ), 0)
    col = lax.broadcasted_iota(jnp.int32, (NY, NZ), 1)
    return row == 0, row == NY - 1, col == 0, col == NZ - 1


def plane_modes(v, y_last, z_last):
    ahead = next_z(v, z_last)
    out = []
    pair = (v + ahead, ahead - v)
    for part in pair:
        above = next_y(part, y_last)
        out.append((part + above, above - part))
    return [out[r][q] for q in range(2) for r in range(2)]


def element_modes(low, high):
    modes = {}
    for comp in range(3):
        for q in range(2):
            for r in range(2):
                a, b = low[4 * comp + 2 * q + r], high[4 * comp + 2 * q + r]
                if q + r > 0:
                    modes[comp, 0, q, r] = a + b
                modes[comp, 1, q, r] = b - a
    return modes


UNIT = ((1, 0, 0), (0, 1, 0), (0, 0, 1))
PAIRS = ((0, 1), (0, 2), (1, 2))


def both(i, j):
    return tuple(UNIT[i][k] + UNIT[j][k] for k in range(3))


BLOCKS = tuple(((i, both(i, j)), (k, both(k, j))) for j in range(3) for i, k in PAIRS if j not in (i, k))
TRIPLE = tuple((i, both(*[k for k in range(3) if k != i])) for i in range(3))


def mode_forces(h):
    out = {}
    trace = (h[(0,) + UNIT[0]] + h[(1,) + UNIT[1]] + h[(2,) + UNIT[2]]) * LAME
    for i in range(3):
        out[(i,) + UNIT[i]] = trace + (2.0 * SHEAR) * h[(i,) + UNIT[i]]
    for i, k in PAIRS:
        shear = SHEAR * (h[(i,) + UNIT[k]] + h[(k,) + UNIT[i]])
        out[(i,) + UNIT[k]] = shear
        out[(k,) + UNIT[i]] = shear
    for (i, a), (k, b) in BLOCKS:
        both_ = (LAME / 3.0) * (h[(i,) + a] + h[(k,) + b])
        out[(i,) + a] = both_ + SHEAR * h[(i,) + a]
        out[(k,) + b] = both_ + SHEAR * h[(k,) + b]
    total = h[(0,) + TRIPLE[0][1]] + h[(1,) + TRIPLE[1][1]] + h[(2,) + TRIPLE[2][1]]
    for i, a in TRIPLE:
        out[(i,) + a] = (SHEAR / 3.0) * (total + h[(i,) + a])
    for i in range(3):
        out[i, 1, 1, 1] = DIAGONAL * h[i, 1, 1, 1]
    return out


def mode_energy(h):
    trace = h[(0,) + UNIT[0]] + h[(1,) + UNIT[1]] + h[(2,) + UNIT[2]]
    summed = LAME * (trace * trace)
    normal = None
    for i in range(3):
        term = h[(i,) + UNIT[i]] * h[(i,) + UNIT[i]]
        normal = term if normal is None else normal + term
    summed = summed + (2.0 * SHEAR) * normal
    shear = None
    for i, k in PAIRS:
        pair = h[(i,) + UNIT[k]] + h[(k,) + UNIT[i]]
        term = pair * pair
        shear = term if shear is None else shear + term
    for (i, a), (k, b) in BLOCKS:
        shear = shear + (h[(i,) + a] * h[(i,) + a] + h[(k,) + b] * h[(k,) + b])
    blocks = None
    for (i, a), (k, b) in BLOCKS:
        pair = h[(i,) + a] + h[(k,) + b]
        term = pair * pair
        blocks = term if blocks is None else blocks + term
    summed = summed + SHEAR * shear + (LAME / 3.0) * blocks
    total = h[(0,) + TRIPLE[0][1]] + h[(1,) + TRIPLE[1][1]] + h[(2,) + TRIPLE[2][1]]
    triple = total * total
    corner = None
    for i, a in TRIPLE:
        triple = triple + h[(i,) + a] * h[(i,) + a]
        term = h[i, 1, 1, 1] * h[i, 1, 1, 1]
        corner = term if corner is None else corner + term
    return summed + (SHEAR / 3.0) * triple + DIAGONAL * corner


def krylov_kernel(slab, table, gathered, basis, moments, rows, weight, inverse, mass, w0, w1, w2, planes, layers):
    first = 2 * slab[0] - 3
    y_first, y_last, z_first, z_last = plane_edges()

    for load in range(LOADS):
        rows[:, 2 * load : 2 * load + 2, :] = gathered[load]

    def set_weight(i, _):
        layer = first - 1 + i
        inside = jnp.where((layer >= 0) & (layer < NX), 1.0, 0.0)
        rho = rows[i]
        weight[i] = (MODE_SCALE * inside) * (void_stiffness + (1.0 - void_stiffness) * (rho * rho * rho))
        return 0

    lax.fori_loop(0, 9, set_weight, 0)

    def set_plane(i, _):
        both_layers = weight[i] + weight[i + 1]
        across = both_layers + prev_y(both_layers, y_first)
        diag = (DIAGONAL / MODE_SCALE) * (across + prev_z(across, z_first))
        code = rows[9 + i]
        inv = jnp.where(code < OUTSIDE - 0.5, 1.0 / diag, 0.0)
        inverse[i] = inv
        mass[i] = diag
        scaled = inv * (1.0 + 2.0 * (first + i).astype(jnp.float32) / (NX - 1))
        for comp in range(3):
            force = jnp.zeros((NY, NZ), jnp.float32)
            for patch in range(PATCHES):
                force = jnp.where(code == float(patch), table[comp, patch], force)
            w0[comp, i] = scaled * force
        return 0

    lax.fori_loop(0, 8, set_plane, 0)

    def shifted_operator(source, target, count, lead):
        def to_modes(i, _):
            for comp in range(3):
                for k, part in enumerate(plane_modes(source[comp, i], y_last, z_last)):
                    planes[i, 4 * comp + k] = part
            return 0

        lax.fori_loop(0, count + 2, to_modes, 0)

        def column(tile, _):
            y = pl.ds(pl.multiple_of(tile * 8, 8), 8)
            for half in range(NZ // 128):
                z = slice(128 * half, 128 * half + 128)
                low = [planes[0, k, y, z] for k in range(12)]
                held = None
                for i in range(count + 1):
                    high = [planes[i + 1, k, y, z] for k in range(12)]
                    e = weight[lead + i, y, z]
                    f = mode_forces(element_modes(low, high))
                    done = {}
                    f = {key: done.setdefault(id(val), val * e) for key, val in f.items()}
                    now = []
                    for comp in range(3):
                        for q in range(2):
                            for r in range(2):
                                k = 4 * comp + 2 * q + r
                                slope = f[comp, 1, q, r]
                                level = f.get((comp, 0, q, r))
                                below = -slope if level is None else level - slope
                                above = slope if level is None else level + slope
                                if held is not None:
                                    layers[i - 1, k, y, z] = held[k] + below
                                now.append(above)
                    held = now
                    low = high
            return 0

        lax.fori_loop(0, NY // 8, column, 0)

        def to_nodes(i, _):
            inv = inverse[lead + i]
            for comp in range(3):
                across = []
                for r in range(2):
                    level, slope = layers[i, 4 * comp + r], layers[i, 4 * comp + 2 + r]
                    across.append((level - slope) + prev_y(level + slope, y_first))
                level, slope = across
                force = (level - slope) + prev_z(level + slope, z_first)
                target[comp, i] = inv * force - source[comp, i + 1]
            return 0

        lax.fori_loop(0, count, to_nodes, 0)

    shifted_operator(w0, w1, 6, 1)
    shifted_operator(w1, w2, 4, 2)

    totals = [jnp.zeros((8, 128), jnp.float32) for _ in range(6)]
    shifted_operator(w2, basis.at[2], 2, 3)
    for i in range(2):
        m = mass[3 + i]
        for comp in range(3):
            v = (w0[comp, 3 + i], w1[comp, 2 + i], w2[comp, 1 + i], basis[2, comp, i])
            mv = [m * a for a in v[:3]]
            products = (mv[0] * v[0], mv[0] * v[1], mv[1] * v[1], mv[1] * v[2], mv[2] * v[2], mv[2] * v[3])
            for k, product in enumerate(products):
                part = product[:, :128] + product[:, 128:]
                totals[k] = totals[k] + ((part[0:8] + part[8:16]) + (part[16:24] + part[24:32]))
    for k in range(6):
        moments[k : k + 1, :] = jnp.sum(totals[k], axis=0, keepdims=True)
    moments[6:8, :] = jnp.zeros((2, 128), jnp.float32)
    basis[0] = w0[:, 3:6]
    basis[1] = w1[:, 2:5]
    basis[2] = w2[:, 1:4]


def step_sizes(nu):
    eta = [nu[k] + nu[k + 1] for k in range(5)]

    def form(v, values):
        summed = None
        for i in range(len(v)):
            for j in range(i, len(v)):
                term = (v[i] * v[j]) * values[i + j]
                term = term if i == j else 2.0 * term
                summed = term if summed is None else summed + term
        return summed

    first = nu[0] / eta[0]
    z = [1.0 - first, -first]
    now = form(z, nu)
    beta = now / nu[0]
    p = [z[0] + beta, z[1]]
    second = now / form(p, eta)
    last = [z[0] - second * p[0], z[1] - second * (p[0] + p[1]), -(second * p[1])]
    then = form(last, nu)
    beta = then / now
    q = [last[0] + beta * p[0], last[1] + beta * p[1], last[2]]
    third = then / form(q, eta)
    return [first + second * p[0] + third * q[0], second * p[1] + third * q[1], third * q[2]]


def combine_kernel(parts, basis, displacement, energies, upper, planes, energy):
    y_first, y_last, z_first, z_last = plane_edges()
    total = parts[0]
    for i in range(1, 16):
        total = total + parts[i]
    nu = [jnp.sum(total[k : k + 1, :], axis=1, keepdims=True) for k in range(6)]
    coefficient = step_sizes(nu)
    wide = [jnp.broadcast_to(c, (NY, NZ)) for c in coefficient]
    for comp in range(3):
        for i in range(3):
            u = wide[0] * basis[0, comp, i] + wide[1] * basis[1, comp, i] + wide[2] * basis[2, comp, i]
            if i < 2:
                displacement[comp, i] = u
            for k, part in enumerate(plane_modes(u, y_last, z_last)):
                planes[i, 4 * comp + k] = part

    def column(tile, _):
        y = pl.ds(pl.multiple_of(tile * 8, 8), 8)
        for half in range(NZ // 128):
            z = slice(128 * half, 128 * half + 128)
            low = [planes[0, k, y, z] for k in range(12)]
            for i in range(2):
                high = [planes[i + 1, k, y, z] for k in range(12)]
                energy[i, y, z] = MODE_SCALE * mode_energy(element_modes(low, high))
                low = high
        return 0

    lax.fori_loop(0, NY // 8, column, 0)
    for load in range(LOADS):
        energies[load] = energy[:, 2 * load : 2 * load + 2, :]


def shards(density, fixed_mask, patch_index, patch_force):
    slab = lax.axis_index("space")
    load = lax.axis_index("load")
    code = jnp.where(fixed_mask == 0, patch_index, int(OUTSIDE)).astype(jnp.float32)
    mine = lax.dynamic_slice_in_dim(code, 2 * load, 2, axis=1)
    own = jnp.stack([density, mine])
    column = lax.all_to_all(jnp.broadcast_to(own[None], (16,) + own.shape), "space", 0, 0, tiled=True)
    rho = jnp.pad(column[:, 0].reshape(NX, 2, NZ), ((4, 4), (0, 0), (0, 0)))
    codes = jnp.pad(column[:, 1].reshape(NX, 2, NZ), ((4, 4), (0, 0), (0, 0)), constant_values=OUTSIDE)
    window = jnp.concatenate(
        [
            lax.dynamic_slice_in_dim(rho, 2 * slab, 9, axis=0),
            lax.dynamic_slice_in_dim(codes, 2 * slab + 1, 8, axis=0),
        ]
    )
    gathered = lax.all_to_all(jnp.broadcast_to(window[None], (16,) + window.shape), "load", 0, 0, tiled=True)

    vmem = pl.BlockSpec(memory_space=pltpu.VMEM)
    smem = pl.BlockSpec(memory_space=pltpu.SMEM)
    field = lambda *shape: pltpu.VMEM(shape + (NY, NZ), jnp.float32)
    basis, moments = pl.pallas_call(
        krylov_kernel,
        out_shape=(
            jax.ShapeDtypeStruct((3, 3, 3, NY, NZ), jnp.float32),
            jax.ShapeDtypeStruct((8, 128), jnp.float32),
        ),
        in_specs=[smem, smem, vmem],
        out_specs=(vmem, vmem),
        scratch_shapes=[field(17), field(9), field(8), field(8), field(3, 8), field(3, 6), field(3, 4), field(8, 12), field(6, 12)],
        name="krylov",
    )(slab.astype(jnp.int32).reshape(1), patch_force[0], gathered)
    parts = lax.all_to_all(jnp.broadcast_to(moments[None], (16, 8, 128)), "space", 0, 0, tiled=True)
    displacement, energies = pl.pallas_call(
        combine_kernel,
        out_shape=(
            jax.ShapeDtypeStruct((3, 2, NY, NZ), jnp.float32),
            jax.ShapeDtypeStruct((LOADS, 2, 2, NZ), jnp.float32),
        ),
        in_specs=[vmem, vmem],
        out_specs=(vmem, vmem),
        scratch_shapes=[field(1), field(3, 12), field(2)],
        name="combine",
    )(parts, basis)
    received = lax.all_to_all(energies, "load", 0, 0, tiled=True)
    summed = jnp.sum(received, axis=0)
    sensitivity = -3.0 * (1.0 - void_stiffness) * density**2 * (summed / LOADS)
    return (displacement[None], sensitivity)


def solution(mesh):
    in_specs = (
        P("space", "load", None),
        P("space", None, None),
        P("space", None, None),
        P("load", None, None),
    )
    out_specs = (P("load", None, "space", None, None), P("space", "load", None))
    return jax.shard_map(shards, mesh=mesh, in_specs=in_specs, out_specs=out_specs, check_vma=False)
```

```python
import jax
import jax.numpy as jnp
from jax import lax
from jax.experimental import pallas as pl
from jax.experimental.pallas import tpu as pltpu
from jax.sharding import PartitionSpec as P

NX, NY, NZ = 32, 32, 256
PATCHES = 16
LOADS = 16
OUTSIDE = 16.0
void_stiffness = 0.001
poisson_ratio = 0.3
LAME = poisson_ratio / ((1.0 + poisson_ratio) * (1.0 - 2.0 * poisson_ratio))
SHEAR = 0.5 / (1.0 + poisson_ratio)
DIAGONAL = (LAME + 4.0 * SHEAR) / 9.0
MODE_SCALE = 1.0 / 16.0


def next_y(v, last):
    return jnp.where(last, 0.0, pltpu.roll(v, v.shape[0] - 1, 0))


def prev_y(v, first):
    return jnp.where(first, 0.0, pltpu.roll(v, 1, 0))


def next_z(v, last):
    return jnp.where(last, 0.0, pltpu.roll(v, v.shape[1] - 1, 1))


def prev_z(v, first):
    return jnp.where(first, 0.0, pltpu.roll(v, 1, 1))


def plane_edges():
    row = lax.broadcasted_iota(jnp.int32, (NY, NZ), 0)
    col = lax.broadcasted_iota(jnp.int32, (NY, NZ), 1)
    return row == 0, row == NY - 1, col == 0, col == NZ - 1


def plane_modes(v, y_last, z_last):
    ahead = next_z(v, z_last)
    out = []
    pair = (v + ahead, ahead - v)
    for part in pair:
        above = next_y(part, y_last)
        out.append((part + above, above - part))
    return [out[r][q] for q in range(2) for r in range(2)]


def element_modes(low, high):
    modes = {}
    for comp in range(3):
        for q in range(2):
            for r in range(2):
                a, b = low[4 * comp + 2 * q + r], high[4 * comp + 2 * q + r]
                if q + r > 0:
                    modes[comp, 0, q, r] = a + b
                modes[comp, 1, q, r] = b - a
    return modes


UNIT = ((1, 0, 0), (0, 1, 0), (0, 0, 1))
PAIRS = ((0, 1), (0, 2), (1, 2))


def both(i, j):
    return tuple(UNIT[i][k] + UNIT[j][k] for k in range(3))


BLOCKS = tuple(((i, both(i, j)), (k, both(k, j))) for j in range(3) for i, k in PAIRS if j not in (i, k))
TRIPLE = tuple((i, both(*[k for k in range(3) if k != i])) for i in range(3))


def mode_forces(h):
    out = {}
    trace = (h[(0,) + UNIT[0]] + h[(1,) + UNIT[1]] + h[(2,) + UNIT[2]]) * LAME
    for i in range(3):
        out[(i,) + UNIT[i]] = trace + (2.0 * SHEAR) * h[(i,) + UNIT[i]]
    for i, k in PAIRS:
        shear = SHEAR * (h[(i,) + UNIT[k]] + h[(k,) + UNIT[i]])
        out[(i,) + UNIT[k]] = shear
        out[(k,) + UNIT[i]] = shear
    for (i, a), (k, b) in BLOCKS:
        both_ = (LAME / 3.0) * (h[(i,) + a] + h[(k,) + b])
        out[(i,) + a] = both_ + SHEAR * h[(i,) + a]
        out[(k,) + b] = both_ + SHEAR * h[(k,) + b]
    total = h[(0,) + TRIPLE[0][1]] + h[(1,) + TRIPLE[1][1]] + h[(2,) + TRIPLE[2][1]]
    for i, a in TRIPLE:
        out[(i,) + a] = (SHEAR / 3.0) * (total + h[(i,) + a])
    for i in range(3):
        out[i, 1, 1, 1] = DIAGONAL * h[i, 1, 1, 1]
    return out


def mode_energy(h):
    trace = h[(0,) + UNIT[0]] + h[(1,) + UNIT[1]] + h[(2,) + UNIT[2]]
    summed = LAME * (trace * trace)
    normal = None
    for i in range(3):
        term = h[(i,) + UNIT[i]] * h[(i,) + UNIT[i]]
        normal = term if normal is None else normal + term
    summed = summed + (2.0 * SHEAR) * normal
    shear = None
    for i, k in PAIRS:
        pair = h[(i,) + UNIT[k]] + h[(k,) + UNIT[i]]
        term = pair * pair
        shear = term if shear is None else shear + term
    for (i, a), (k, b) in BLOCKS:
        shear = shear + (h[(i,) + a] * h[(i,) + a] + h[(k,) + b] * h[(k,) + b])
    blocks = None
    for (i, a), (k, b) in BLOCKS:
        pair = h[(i,) + a] + h[(k,) + b]
        term = pair * pair
        blocks = term if blocks is None else blocks + term
    summed = summed + SHEAR * shear + (LAME / 3.0) * blocks
    total = h[(0,) + TRIPLE[0][1]] + h[(1,) + TRIPLE[1][1]] + h[(2,) + TRIPLE[2][1]]
    triple = total * total
    corner = None
    for i, a in TRIPLE:
        triple = triple + h[(i,) + a] * h[(i,) + a]
        term = h[i, 1, 1, 1] * h[i, 1, 1, 1]
        corner = term if corner is None else corner + term
    return summed + (SHEAR / 3.0) * triple + DIAGONAL * corner


def krylov_kernel(place, table, codes, *refs):
    pieces, (basis, moments, staged, rows, weight, inverse, mass, w0, w1, planes, layers) = refs[:4], refs[4:]
    own = place[1]
    first = 2 * place[0] - 2
    y_first, y_last, z_first, z_last = plane_edges()

    for far in range(4):
        for near in range(4):
            staged[own ^ (4 * far + near)] = pieces[far][near]
    for load in range(LOADS):
        rows[:, 2 * load : 2 * load + 2, :] = staged[load]

    def set_weight(i, _):
        layer = first - 1 + i
        inside = jnp.where((layer >= 0) & (layer < NX), 1.0, 0.0)
        rho = rows[i]
        weight[i] = (MODE_SCALE * inside) * (void_stiffness + (1.0 - void_stiffness) * (rho * rho * rho))
        return 0

    lax.fori_loop(0, 8, set_weight, 0)

    def set_plane(i, code):
        both_layers = weight[i] + weight[i + 1]
        across = both_layers + prev_y(both_layers, y_first)
        diag = (DIAGONAL / MODE_SCALE) * (across + prev_z(across, z_first))
        inv = jnp.where(code < OUTSIDE - 0.5, 1.0 / diag, 0.0)
        inverse[i] = inv
        mass[i] = diag
        scaled = inv * (1.0 + 2.0 * (first + i).astype(jnp.float32) / (NX - 1))
        force = [jnp.zeros((NY, NZ), jnp.float32) for _ in range(3)]
        for patch in range(PATCHES):
            here = code == float(patch)
            force = [jnp.where(here, table[comp, patch], force[comp]) for comp in range(3)]
        for comp in range(3):
            w0[comp, i] = scaled * force[comp]

    lax.fori_loop(0, 2, lambda i, _: (set_plane(i, rows[8 + i]), 0)[1], 0)
    lax.fori_loop(2, 4, lambda i, _: (set_plane(i, codes[i - 2]), 0)[1], 0)
    lax.fori_loop(4, 7, lambda i, _: (set_plane(i, rows[6 + i]), 0)[1], 0)

    def to_modes(source, count):
        def body(i, _):
            for comp in range(3):
                for k, part in enumerate(plane_modes(source[comp, i], y_last, z_last)):
                    planes[i, 4 * comp + k] = part
            return 0

        lax.fori_loop(0, count, body, 0)

    def shifted_operator(source, target, count, lead):
        to_modes(source, count + 2)

        def column(tile, _):
            y = pl.ds(pl.multiple_of(tile * 8, 8), 8)
            for half in range(NZ // 128):
                z = slice(128 * half, 128 * half + 128)
                low = [planes[0, k, y, z] for k in range(12)]
                held = None
                for i in range(count + 1):
                    high = [planes[i + 1, k, y, z] for k in range(12)]
                    e = weight[lead + i, y, z]
                    f = mode_forces(element_modes(low, high))
                    done = {}
                    f = {key: done.setdefault(id(val), val * e) for key, val in f.items()}
                    now = []
                    for comp in range(3):
                        for q in range(2):
                            for r in range(2):
                                k = 4 * comp + 2 * q + r
                                slope = f[comp, 1, q, r]
                                level = f.get((comp, 0, q, r))
                                below = -slope if level is None else level - slope
                                above = slope if level is None else level + slope
                                if held is not None:
                                    layers[i - 1, k, y, z] = held[k] + below
                                now.append(above)
                    held = now
                    low = high
            return 0

        lax.fori_loop(0, NY // 8, column, 0)

        def to_nodes(i, _):
            inv = inverse[lead + i]
            for comp in range(3):
                across = []
                for r in range(2):
                    level, slope = layers[i, 4 * comp + r], layers[i, 4 * comp + 2 + r]
                    across.append((level - slope) + prev_y(level + slope, y_first))
                level, slope = across
                force = (level - slope) + prev_z(level + slope, z_first)
                target[comp, i] = inv * force - source[comp, i + 1]
            return 0

        lax.fori_loop(0, count, to_nodes, 0)

    shifted_operator(w0, w1, 5, 1)
    shifted_operator(w1, basis.at[2], 3, 2)
    basis[0] = w0[:, 2:5]
    basis[1] = w1[:, 1:4]

    to_modes(basis.at[2], 3)

    def column(tile, summed):
        y = pl.ds(pl.multiple_of(tile * 8, 8), 8)
        for half in range(NZ // 128):
            z = slice(128 * half, 128 * half + 128)
            low = [planes[0, k, y, z] for k in range(12)]
            for i in range(2):
                high = [planes[i + 1, k, y, z] for k in range(12)]
                summed = summed + weight[3 + i, y, z] * mode_energy(element_modes(low, high))
                low = high
        return summed

    totals = [jnp.zeros((8, 128), jnp.float32) for _ in range(5)]
    totals.append(lax.fori_loop(0, NY // 8, column, jnp.zeros((8, 128), jnp.float32)))
    for i in range(2):
        m = mass[2 + i]
        for comp in range(3):
            v = [basis[k, comp, i] for k in range(3)]
            mv = [m * a for a in v]
            products = (mv[0] * v[0], mv[0] * v[1], mv[1] * v[1], mv[1] * v[2], mv[2] * v[2])
            for k, product in enumerate(products):
                part = product[:, :128] + product[:, 128:]
                totals[k] = totals[k] + ((part[0:8] + part[8:16]) + (part[16:24] + part[24:32]))
    sums = [jnp.sum(total, axis=0, keepdims=True) for total in totals]
    block = jnp.concatenate(sums + [jnp.zeros((2, 128), jnp.float32)], axis=0)
    for i in range(16):
        moments[i] = block


def step_sizes(nu):
    eta = [nu[k] + nu[k + 1] for k in range(4)] + [nu[5]]

    def form(v, values):
        summed = None
        for i in range(len(v)):
            for j in range(i, len(v)):
                term = (v[i] * v[j]) * values[i + j]
                term = term if i == j else 2.0 * term
                summed = term if summed is None else summed + term
        return summed

    first = nu[0] / eta[0]
    z = [1.0 - first, -first]
    now = form(z, nu)
    beta = now / nu[0]
    p = [z[0] + beta, z[1]]
    second = now / form(p, eta)
    last = [z[0] - second * p[0], z[1] - second * (p[0] + p[1]), -(second * p[1])]
    then = form(last, nu)
    beta = then / now
    q = [last[0] + beta * p[0], last[1] + beta * p[1], last[2]]
    third = then / form(q, eta)
    return [first + second * p[0] + third * q[0], second * p[1] + third * q[1], third * q[2]]


def combine_kernel(parts, basis, displacement, energies, planes, energy):
    y_first, y_last, z_first, z_last = plane_edges()
    total = parts[0]
    for i in range(1, 16):
        total = total + parts[i]
    nu = [jnp.sum(total[k : k + 1, :], axis=1, keepdims=True) for k in range(6)]
    coefficient = step_sizes(nu)
    wide = [jnp.broadcast_to(c, (NY, NZ)) for c in coefficient]
    for comp in range(3):
        for i in range(3):
            u = wide[0] * basis[0, comp, i] + wide[1] * basis[1, comp, i] + wide[2] * basis[2, comp, i]
            if i < 2:
                displacement[comp, i] = u
            for k, part in enumerate(plane_modes(u, y_last, z_last)):
                planes[i, 4 * comp + k] = part

    def column(tile, _):
        y = pl.ds(pl.multiple_of(tile * 8, 8), 8)
        for half in range(NZ // 128):
            z = slice(128 * half, 128 * half + 128)
            low = [planes[0, k, y, z] for k in range(12)]
            for i in range(2):
                high = [planes[i + 1, k, y, z] for k in range(12)]
                energy[i, y, z] = MODE_SCALE * mode_energy(element_modes(low, high))
                low = high
        return 0

    lax.fori_loop(0, NY // 8, column, 0)
    for load in range(LOADS):
        energies[load] = energy[:, 2 * load : 2 * load + 2, :]


def others(x, distance):
    return [lax.ppermute(x, "load", [(i, i ^ (k * distance)) for i in range(LOADS)]) for k in range(1, 4)]


def shards(density, fixed_mask, patch_index, patch_force):
    slab = lax.axis_index("space")
    load = lax.axis_index("load")
    code = jnp.where(fixed_mask == 0, patch_index, int(OUTSIDE)).astype(jnp.float32)
    mine = lax.dynamic_slice_in_dim(code, 2 * load, 2, axis=1)
    own = jnp.stack([density, mine])
    column = lax.all_to_all(jnp.broadcast_to(own[None], (16,) + own.shape), "space", 0, 0, tiled=True)
    rho = jnp.pad(column[:, 0].reshape(NX, 2, NZ), ((3, 3), (0, 0), (0, 0)))
    codes = jnp.pad(column[:, 1].reshape(NX, 2, NZ), ((2, 3), (0, 0), (0, 0)), constant_values=OUTSIDE)
    near = lax.dynamic_slice_in_dim(codes, 2 * slab, 7, axis=0)
    window = jnp.concatenate([lax.dynamic_slice_in_dim(rho, 2 * slab, 8, axis=0), near[:2], near[4:]])
    line = jnp.stack([window] + others(window, 1))
    pieces = [line] + others(line, 4)

    vmem = pl.BlockSpec(memory_space=pltpu.VMEM)
    smem = pl.BlockSpec(memory_space=pltpu.SMEM)
    field = lambda *shape: pltpu.VMEM(shape + (NY, NZ), jnp.float32)
    basis, moments = pl.pallas_call(
        krylov_kernel,
        out_shape=(
            jax.ShapeDtypeStruct((3, 3, 3, NY, NZ), jnp.float32),
            jax.ShapeDtypeStruct((16, 8, 128), jnp.float32),
        ),
        in_specs=[smem, smem, vmem] + [vmem] * 4,
        out_specs=(vmem, vmem),
        scratch_shapes=[pltpu.VMEM((LOADS, 13, 2, NZ), jnp.float32)]
        + [field(13), field(8), field(7), field(7), field(3, 7), field(3, 5), field(7, 12), field(5, 12)],
        name="krylov",
    )(jnp.stack([slab, load]).astype(jnp.int32), patch_force[0], code, *pieces)
    parts = lax.all_to_all(moments, "space", 0, 0, tiled=True)
    displacement, energies = pl.pallas_call(
        combine_kernel,
        out_shape=(
            jax.ShapeDtypeStruct((3, 2, NY, NZ), jnp.float32),
            jax.ShapeDtypeStruct((LOADS, 2, 2, NZ), jnp.float32),
        ),
        in_specs=[vmem, vmem],
        out_specs=(vmem, vmem),
        scratch_shapes=[field(3, 12), field(2)],
        name="combine",
    )(parts, basis)
    received = lax.all_to_all(energies, "load", 0, 0, tiled=True)
    summed = jnp.sum(received, axis=0)
    sensitivity = -3.0 * (1.0 - void_stiffness) * density**2 * (summed / LOADS)
    return (displacement[None], sensitivity)


def solution(mesh):
    in_specs = (
        P("space", "load", None),
        P("space", None, None),
        P("space", None, None),
        P("load", None, None),
    )
    out_specs = (P("load", None, "space", None, None), P("space", "load", None))
    return jax.shard_map(shards, mesh=mesh, in_specs=in_specs, out_specs=out_specs, check_vma=False)
```

```python
import jax
import jax.numpy as jnp
from jax import lax
from jax.experimental import pallas as pl
from jax.experimental.pallas import tpu as pltpu
from jax.sharding import PartitionSpec as P

NX, NY, NZ = 32, 32, 256
PATCHES = 16
LOADS = 16
void_stiffness = 0.001
poisson_ratio = 0.3
LAME = poisson_ratio / ((1.0 + poisson_ratio) * (1.0 - 2.0 * poisson_ratio))
SHEAR = 0.5 / (1.0 + poisson_ratio)
DIAGONAL = (LAME + 4.0 * SHEAR) / 9.0
MODE_SCALE = 1.0 / 16.0


def next_y(v, last):
    return jnp.where(last, 0.0, pltpu.roll(v, v.shape[0] - 1, 0))


def prev_y(v, first):
    return jnp.where(first, 0.0, pltpu.roll(v, 1, 0))


def next_z(v, last):
    return jnp.where(last, 0.0, pltpu.roll(v, v.shape[1] - 1, 1))


def prev_z(v, first):
    return jnp.where(first, 0.0, pltpu.roll(v, 1, 1))


def plane_edges():
    row = lax.broadcasted_iota(jnp.int32, (NY, NZ), 0)
    col = lax.broadcasted_iota(jnp.int32, (NY, NZ), 1)
    return row == 0, row == NY - 1, col == 0, col == NZ - 1


def plane_modes(v, y_last, z_last):
    ahead = next_z(v, z_last)
    out = []
    pair = (v + ahead, ahead - v)
    for part in pair:
        above = next_y(part, y_last)
        out.append((part + above, above - part))
    return [out[r][q] for q in range(2) for r in range(2)]


def element_modes(low, high):
    modes = {}
    for comp in range(3):
        for q in range(2):
            for r in range(2):
                a, b = low[4 * comp + 2 * q + r], high[4 * comp + 2 * q + r]
                if q + r > 0:
                    modes[comp, 0, q, r] = a + b
                modes[comp, 1, q, r] = b - a
    return modes


UNIT = ((1, 0, 0), (0, 1, 0), (0, 0, 1))
PAIRS = ((0, 1), (0, 2), (1, 2))


def both(i, j):
    return tuple(UNIT[i][k] + UNIT[j][k] for k in range(3))


BLOCKS = tuple(((i, both(i, j)), (k, both(k, j))) for j in range(3) for i, k in PAIRS if j not in (i, k))
TRIPLE = tuple((i, both(*[k for k in range(3) if k != i])) for i in range(3))


def mode_forces(h):
    out = {}
    trace = (h[(0,) + UNIT[0]] + h[(1,) + UNIT[1]] + h[(2,) + UNIT[2]]) * LAME
    for i in range(3):
        out[(i,) + UNIT[i]] = trace + (2.0 * SHEAR) * h[(i,) + UNIT[i]]
    for i, k in PAIRS:
        shear = SHEAR * (h[(i,) + UNIT[k]] + h[(k,) + UNIT[i]])
        out[(i,) + UNIT[k]] = shear
        out[(k,) + UNIT[i]] = shear
    for (i, a), (k, b) in BLOCKS:
        both_ = (LAME / 3.0) * (h[(i,) + a] + h[(k,) + b])
        out[(i,) + a] = both_ + SHEAR * h[(i,) + a]
        out[(k,) + b] = both_ + SHEAR * h[(k,) + b]
    total = h[(0,) + TRIPLE[0][1]] + h[(1,) + TRIPLE[1][1]] + h[(2,) + TRIPLE[2][1]]
    for i, a in TRIPLE:
        out[(i,) + a] = (SHEAR / 3.0) * (total + h[(i,) + a])
    for i in range(3):
        out[i, 1, 1, 1] = DIAGONAL * h[i, 1, 1, 1]
    return out


def mode_energy(h):
    trace = h[(0,) + UNIT[0]] + h[(1,) + UNIT[1]] + h[(2,) + UNIT[2]]
    summed = LAME * (trace * trace)
    normal = None
    for i in range(3):
        term = h[(i,) + UNIT[i]] * h[(i,) + UNIT[i]]
        normal = term if normal is None else normal + term
    summed = summed + (2.0 * SHEAR) * normal
    shear = None
    for i, k in PAIRS:
        pair = h[(i,) + UNIT[k]] + h[(k,) + UNIT[i]]
        term = pair * pair
        shear = term if shear is None else shear + term
    for (i, a), (k, b) in BLOCKS:
        shear = shear + (h[(i,) + a] * h[(i,) + a] + h[(k,) + b] * h[(k,) + b])
    blocks = None
    for (i, a), (k, b) in BLOCKS:
        pair = h[(i,) + a] + h[(k,) + b]
        term = pair * pair
        blocks = term if blocks is None else blocks + term
    summed = summed + SHEAR * shear + (LAME / 3.0) * blocks
    total = h[(0,) + TRIPLE[0][1]] + h[(1,) + TRIPLE[1][1]] + h[(2,) + TRIPLE[2][1]]
    triple = total * total
    corner = None
    for i, a in TRIPLE:
        triple = triple + h[(i,) + a] * h[(i,) + a]
        term = h[i, 1, 1, 1] * h[i, 1, 1, 1]
        corner = term if corner is None else corner + term
    return summed + (SHEAR / 3.0) * triple + DIAGONAL * corner


def krylov_kernel(place, table, fixed, patches, *refs):
    pieces, (basis, moments, staged, rows, weight, inverse, mass, w0, w1, planes, layers) = refs[:4], refs[4:]
    own = place[1]
    first = 2 * place[0] - 2
    y_first, y_last, z_first, z_last = plane_edges()

    for far in range(4):
        for near in range(4):
            staged[own ^ (4 * far + near)] = pieces[far][near]
    for load in range(LOADS):
        rows[:, 2 * load : 2 * load + 2, :] = staged[load]

    def set_weight(i, _):
        layer = first - 1 + i
        inside = jnp.where((layer >= 0) & (layer < NX), 1.0, 0.0)
        rho = rows[i]
        weight[i] = (MODE_SCALE * inside) * (void_stiffness + (1.0 - void_stiffness) * (rho * rho * rho))
        return 0

    lax.fori_loop(0, 8, set_weight, 0)

    def set_plane(i, code):
        both_layers = weight[i] + weight[i + 1]
        across = both_layers + prev_y(both_layers, y_first)
        diag = (DIAGONAL / MODE_SCALE) * (across + prev_z(across, z_first))
        inv = jnp.where(code > 0.5, 1.0 / diag, 0.0)
        inverse[i] = inv
        mass[i] = diag
        scaled = inv * (1.0 + 2.0 * (first + i).astype(jnp.float32) / (NX - 1))
        force = [jnp.zeros((NY, NZ), jnp.float32) for _ in range(3)]
        for patch in range(PATCHES):
            here = code == float(patch + 1)
            force = [jnp.where(here, table[comp, patch], force[comp]) for comp in range(3)]
        for comp in range(3):
            w0[comp, i] = scaled * force[comp]

    lax.fori_loop(0, 2, lambda i, _: (set_plane(i, rows[8 + i]), 0)[1], 0)
    lax.fori_loop(2, 4, lambda i, _: (set_plane(i, jnp.where(fixed[i - 2] == 0, patches[i - 2] + 1, 0).astype(jnp.float32)), 0)[1], 0)
    lax.fori_loop(4, 7, lambda i, _: (set_plane(i, rows[6 + i]), 0)[1], 0)

    def to_modes(source, count):
        def body(i, _):
            for comp in range(3):
                for k, part in enumerate(plane_modes(source[comp, i], y_last, z_last)):
                    planes[i, 4 * comp + k] = part
            return 0

        lax.fori_loop(0, count, body, 0)

    def shifted_operator(source, target, count, lead):
        to_modes(source, count + 2)

        def column(tile, _):
            y = pl.ds(pl.multiple_of(tile * 8, 8), 8)
            for half in range(NZ // 128):
                z = slice(128 * half, 128 * half + 128)
                low = [planes[0, k, y, z] for k in range(12)]
                held = None
                for i in range(count + 1):
                    high = [planes[i + 1, k, y, z] for k in range(12)]
                    e = weight[lead + i, y, z]
                    f = mode_forces(element_modes(low, high))
                    done = {}
                    f = {key: done.setdefault(id(val), val * e) for key, val in f.items()}
                    now = []
                    for comp in range(3):
                        for q in range(2):
                            for r in range(2):
                                k = 4 * comp + 2 * q + r
                                slope = f[comp, 1, q, r]
                                level = f.get((comp, 0, q, r))
                                below = -slope if level is None else level - slope
                                above = slope if level is None else level + slope
                                if held is not None:
                                    layers[i - 1, k, y, z] = held[k] + below
                                now.append(above)
                    held = now
                    low = high
            return 0

        lax.fori_loop(0, NY // 8, column, 0)

        def to_nodes(i, _):
            inv = inverse[lead + i]
            for comp in range(3):
                across = []
                for r in range(2):
                    level, slope = layers[i, 4 * comp + r], layers[i, 4 * comp + 2 + r]
                    across.append((level - slope) + prev_y(level + slope, y_first))
                level, slope = across
                force = (level - slope) + prev_z(level + slope, z_first)
                target[comp, i] = inv * force - source[comp, i + 1]
            return 0

        lax.fori_loop(0, count, to_nodes, 0)

    shifted_operator(w0, w1, 5, 1)
    shifted_operator(w1, basis.at[2], 3, 2)
    basis[0] = w0[:, 2:5]
    basis[1] = w1[:, 1:4]

    to_modes(basis.at[2], 3)

    def column(tile, summed):
        y = pl.ds(pl.multiple_of(tile * 8, 8), 8)
        for half in range(NZ // 128):
            z = slice(128 * half, 128 * half + 128)
            low = [planes[0, k, y, z] for k in range(12)]
            for i in range(2):
                high = [planes[i + 1, k, y, z] for k in range(12)]
                summed = summed + weight[3 + i, y, z] * mode_energy(element_modes(low, high))
                low = high
        return summed

    totals = [jnp.zeros((8, 128), jnp.float32) for _ in range(5)]
    totals.append(lax.fori_loop(0, NY // 8, column, jnp.zeros((8, 128), jnp.float32)))
    for i in range(2):
        m = mass[2 + i]
        for comp in range(3):
            v = [basis[k, comp, i] for k in range(3)]
            mv = [m * a for a in v]
            products = (mv[0] * v[0], mv[0] * v[1], mv[1] * v[1], mv[1] * v[2], mv[2] * v[2])
            for k, product in enumerate(products):
                part = product[:, :128] + product[:, 128:]
                totals[k] = totals[k] + ((part[0:8] + part[8:16]) + (part[16:24] + part[24:32]))
    sums = [jnp.sum(total, axis=0, keepdims=True) for total in totals]
    block = jnp.concatenate(sums + [jnp.zeros((2, 128), jnp.float32)], axis=0)
    for i in range(16):
        moments[i] = block


def step_sizes(nu):
    eta = [nu[k] + nu[k + 1] for k in range(4)] + [nu[5]]

    def form(v, values):
        summed = None
        for i in range(len(v)):
            for j in range(i, len(v)):
                term = (v[i] * v[j]) * values[i + j]
                term = term if i == j else 2.0 * term
                summed = term if summed is None else summed + term
        return summed

    first = nu[0] / eta[0]
    z = [1.0 - first, -first]
    now = form(z, nu)
    beta = now / nu[0]
    p = [z[0] + beta, z[1]]
    second = now / form(p, eta)
    last = [z[0] - second * p[0], z[1] - second * (p[0] + p[1]), -(second * p[1])]
    then = form(last, nu)
    beta = then / now
    q = [last[0] + beta * p[0], last[1] + beta * p[1], last[2]]
    third = then / form(q, eta)
    return [first + second * p[0] + third * q[0], second * p[1] + third * q[1], third * q[2]]


def combine_kernel(parts, basis, displacement, energies, planes, energy):
    y_first, y_last, z_first, z_last = plane_edges()
    total = parts[0]
    for i in range(1, 16):
        total = total + parts[i]
    nu = [jnp.sum(total[k : k + 1, :], axis=1, keepdims=True) for k in range(6)]
    coefficient = step_sizes(nu)
    wide = [jnp.broadcast_to(c, (NY, NZ)) for c in coefficient]
    for comp in range(3):
        for i in range(3):
            u = wide[0] * basis[0, comp, i] + wide[1] * basis[1, comp, i] + wide[2] * basis[2, comp, i]
            if i < 2:
                displacement[comp, i] = u
            for k, part in enumerate(plane_modes(u, y_last, z_last)):
                planes[i, 4 * comp + k] = part

    def column(tile, _):
        y = pl.ds(pl.multiple_of(tile * 8, 8), 8)
        for half in range(NZ // 128):
            z = slice(128 * half, 128 * half + 128)
            low = [planes[0, k, y, z] for k in range(12)]
            for i in range(2):
                high = [planes[i + 1, k, y, z] for k in range(12)]
                energy[i, y, z] = MODE_SCALE * mode_energy(element_modes(low, high))
                low = high
        return 0

    lax.fori_loop(0, NY // 8, column, 0)
    for load in range(LOADS):
        energies[load] = energy[:, 2 * load : 2 * load + 2, :]


def others(x, distance):
    return [lax.ppermute(x, "load", [(i, i ^ (k * distance)) for i in range(LOADS)]) for k in range(1, 4)]


def shards(density, fixed_mask, patch_index, patch_force):
    slab = lax.axis_index("space")
    load = lax.axis_index("load")
    core = slab % 2
    fixed_rows = lax.dynamic_slice_in_dim(fixed_mask, 2 * load, 2, axis=1)
    patch_rows = lax.dynamic_slice_in_dim(patch_index, 2 * load, 2, axis=1)
    mine = jnp.where(fixed_rows == 0, patch_rows + 1, 0).astype(jnp.float32)
    own = jnp.stack([density, mine], 1)
    partner = lax.ppermute(own, "space", [(i, i ^ 1) for i in range(16)])
    chip = jnp.concatenate([jnp.where(core == 0, own, partner), jnp.where(core == 0, partner, own)])
    below = lax.ppermute(chip, "space", [(i, i + 2) for i in range(14)])
    above = lax.ppermute(chip, "space", [(i + 2, i) for i in range(14)])
    lane = jnp.concatenate([below, chip, above])
    lane = lax.dynamic_slice_in_dim(lane, 1 + 2 * core, 8, axis=0)
    window = jnp.concatenate([lane[:, 0], lane[1:3, 1], lane[5:, 1]])
    line = jnp.stack([window] + others(window, 1))
    pieces = [line] + others(line, 4)

    vmem = pl.BlockSpec(memory_space=pltpu.VMEM)
    smem = pl.BlockSpec(memory_space=pltpu.SMEM)
    field = lambda *shape: pltpu.VMEM(shape + (NY, NZ), jnp.float32)
    basis, moments = pl.pallas_call(
        krylov_kernel,
        out_shape=(
            jax.ShapeDtypeStruct((3, 3, 3, NY, NZ), jnp.float32),
            jax.ShapeDtypeStruct((16, 8, 128), jnp.float32),
        ),
        in_specs=[smem, smem, vmem, vmem] + [vmem] * 4,
        out_specs=(vmem, vmem),
        scratch_shapes=[pltpu.VMEM((LOADS, 13, 2, NZ), jnp.float32)]
        + [field(13), field(8), field(7), field(7), field(3, 7), field(3, 5), field(7, 12), field(5, 12)],
        compiler_params=pltpu.CompilerParams(vmem_limit_bytes=12 << 20),
        name="krylov",
    )(jnp.stack([slab, load]).astype(jnp.int32), patch_force[0], fixed_mask, patch_index, *pieces)
    parts = lax.all_to_all(moments, "space", 0, 0, tiled=True)
    displacement, energies = pl.pallas_call(
        combine_kernel,
        out_shape=(
            jax.ShapeDtypeStruct((3, 2, NY, NZ), jnp.float32),
            jax.ShapeDtypeStruct((LOADS, 2, 2, NZ), jnp.float32),
        ),
        in_specs=[vmem, vmem],
        out_specs=(vmem, vmem),
        scratch_shapes=[field(3, 12), field(2)],
        compiler_params=pltpu.CompilerParams(vmem_limit_bytes=6 << 20),
        name="combine",
    )(parts, basis)
    received = lax.all_to_all(energies, "load", 0, 0, tiled=True)
    summed = jnp.sum(received, axis=0)
    sensitivity = -3.0 * (1.0 - void_stiffness) * density**2 * (summed / LOADS)
    return (displacement[None], sensitivity)


def solution(mesh):
    in_specs = (
        P("space", "load", None),
        P("space", None, None),
        P("space", None, None),
        P("load", None, None),
    )
    out_specs = (P("load", None, "space", None, None), P("space", "load", None))
    return jax.shard_map(shards, mesh=mesh, in_specs=in_specs, out_specs=out_specs, check_vma=False)
```

```python
import jax
import jax.numpy as jnp
from jax import lax
from jax.experimental import pallas as pl
from jax.experimental.pallas import tpu as pltpu
from jax.sharding import PartitionSpec as P

NX, NY, NZ = 32, 32, 256
PATCHES = 16
LOADS = 16
void_stiffness = 0.001
poisson_ratio = 0.3
LAME = poisson_ratio / ((1.0 + poisson_ratio) * (1.0 - 2.0 * poisson_ratio))
SHEAR = 0.5 / (1.0 + poisson_ratio)
DIAGONAL = (LAME + 4.0 * SHEAR) / 9.0
MODE_SCALE = 1.0 / 16.0


def next_y(v, last):
    return jnp.where(last, 0.0, pltpu.roll(v, v.shape[0] - 1, 0))


def prev_y(v, first):
    return jnp.where(first, 0.0, pltpu.roll(v, 1, 0))


def next_z(v, last):
    return jnp.where(last, 0.0, pltpu.roll(v, v.shape[1] - 1, 1))


def prev_z(v, first):
    return jnp.where(first, 0.0, pltpu.roll(v, 1, 1))


def plane_edges():
    row = lax.broadcasted_iota(jnp.int32, (NY, NZ), 0)
    col = lax.broadcasted_iota(jnp.int32, (NY, NZ), 1)
    return row == 0, row == NY - 1, col == 0, col == NZ - 1


def plane_modes(v, y_last, z_last):
    ahead = next_z(v, z_last)
    out = []
    pair = (v + ahead, ahead - v)
    for part in pair:
        above = next_y(part, y_last)
        out.append((part + above, above - part))
    return [out[r][q] for q in range(2) for r in range(2)]


def element_modes(low, high):
    modes = {}
    for comp in range(3):
        for q in range(2):
            for r in range(2):
                a, b = low[4 * comp + 2 * q + r], high[4 * comp + 2 * q + r]
                if q + r > 0:
                    modes[comp, 0, q, r] = a + b
                modes[comp, 1, q, r] = b - a
    return modes


UNIT = ((1, 0, 0), (0, 1, 0), (0, 0, 1))
PAIRS = ((0, 1), (0, 2), (1, 2))


def both(i, j):
    return tuple(UNIT[i][k] + UNIT[j][k] for k in range(3))


BLOCKS = tuple(((i, both(i, j)), (k, both(k, j))) for j in range(3) for i, k in PAIRS if j not in (i, k))
TRIPLE = tuple((i, both(*[k for k in range(3) if k != i])) for i in range(3))


def mode_forces(h):
    out = {}
    trace = (h[(0,) + UNIT[0]] + h[(1,) + UNIT[1]] + h[(2,) + UNIT[2]]) * LAME
    for i in range(3):
        out[(i,) + UNIT[i]] = trace + (2.0 * SHEAR) * h[(i,) + UNIT[i]]
    for i, k in PAIRS:
        shear = SHEAR * (h[(i,) + UNIT[k]] + h[(k,) + UNIT[i]])
        out[(i,) + UNIT[k]] = shear
        out[(k,) + UNIT[i]] = shear
    for (i, a), (k, b) in BLOCKS:
        both_ = (LAME / 3.0) * (h[(i,) + a] + h[(k,) + b])
        out[(i,) + a] = both_ + SHEAR * h[(i,) + a]
        out[(k,) + b] = both_ + SHEAR * h[(k,) + b]
    total = h[(0,) + TRIPLE[0][1]] + h[(1,) + TRIPLE[1][1]] + h[(2,) + TRIPLE[2][1]]
    for i, a in TRIPLE:
        out[(i,) + a] = (SHEAR / 3.0) * (total + h[(i,) + a])
    for i in range(3):
        out[i, 1, 1, 1] = DIAGONAL * h[i, 1, 1, 1]
    return out


def mode_energy(h):
    trace = h[(0,) + UNIT[0]] + h[(1,) + UNIT[1]] + h[(2,) + UNIT[2]]
    summed = LAME * (trace * trace)
    normal = None
    for i in range(3):
        term = h[(i,) + UNIT[i]] * h[(i,) + UNIT[i]]
        normal = term if normal is None else normal + term
    summed = summed + (2.0 * SHEAR) * normal
    shear = None
    for i, k in PAIRS:
        pair = h[(i,) + UNIT[k]] + h[(k,) + UNIT[i]]
        term = pair * pair
        shear = term if shear is None else shear + term
    for (i, a), (k, b) in BLOCKS:
        shear = shear + (h[(i,) + a] * h[(i,) + a] + h[(k,) + b] * h[(k,) + b])
    blocks = None
    for (i, a), (k, b) in BLOCKS:
        pair = h[(i,) + a] + h[(k,) + b]
        term = pair * pair
        blocks = term if blocks is None else blocks + term
    summed = summed + SHEAR * shear + (LAME / 3.0) * blocks
    total = h[(0,) + TRIPLE[0][1]] + h[(1,) + TRIPLE[1][1]] + h[(2,) + TRIPLE[2][1]]
    triple = total * total
    corner = None
    for i, a in TRIPLE:
        triple = triple + h[(i,) + a] * h[(i,) + a]
        term = h[i, 1, 1, 1] * h[i, 1, 1, 1]
        corner = term if corner is None else corner + term
    return summed + (SHEAR / 3.0) * triple + DIAGONAL * corner


def code_of(fixed, patch):
    return jnp.where(fixed == 0, patch + 1, 0).astype(jnp.float32)


def pack_kernel(gathered, density, fixed, patches, own, upper, lower, factor, rows):
    for load in range(LOADS):
        rows[:, 2 * load : 2 * load + 2, :] = gathered[load]
    for i in range(2):
        rho = rows[i]
        layer = MODE_SCALE * (void_stiffness + (1.0 - void_stiffness) * (rho * rho * rho))
        code = code_of(fixed[i], patches[i])
        own[1 - i] = layer
        own[2 + i] = code
        if i == 0:
            lower[0] = layer
            lower[1] = code
        else:
            upper[0] = layer
    mine = density[...]
    factor[...] = (-3.0 * (1.0 - void_stiffness) / LOADS) * (mine * mine)


def krylov_kernel(place, table, own, below, above, below_next, above_next, basis, moments, *scratch):
    weight, codes, inverse, mass, w0, w1, planes, layers = scratch
    first = 2 * place[0] - 2
    y_first, y_last, z_first, z_last = plane_edges()

    layer_list = [(below_next, 0), (below, 1), (below, 0), (own, 1), (own, 0), (above, 1), (above, 0), (above_next, 0)]
    code_list = [(below, 2), (below, 3), (own, 2), (own, 3), (above, 2), (above, 3), (above_next, 1)]
    for target, offset, refs in ((weight, first - 1, layer_list), (codes, first, code_list)):
        for i, (ref, k) in enumerate(refs):
            inside = (offset + i >= 0) & (offset + i < NX)
            target[i] = ref[k] if ref is own else ref[k] * jnp.where(inside, 1.0, 0.0)

    def set_plane(i, _):
        code = codes[i]
        both_layers = weight[i] + weight[i + 1]
        across = both_layers + prev_y(both_layers, y_first)
        diag = (DIAGONAL / MODE_SCALE) * (across + prev_z(across, z_first))
        inv = jnp.where(code > 0.5, 1.0 / diag, 0.0)
        inverse[i] = inv
        mass[i] = diag
        scaled = inv * (1.0 + 2.0 * (first + i).astype(jnp.float32) / (NX - 1))
        force = [jnp.zeros((NY, NZ), jnp.float32) for _ in range(3)]
        for patch in range(PATCHES):
            here = code == float(patch + 1)
            force = [jnp.where(here, table[comp, patch], force[comp]) for comp in range(3)]
        for comp in range(3):
            w0[comp, i] = scaled * force[comp]
        return 0

    lax.fori_loop(0, 7, set_plane, 0)

    def to_modes(source, count):
        def body(i, _):
            for comp in range(3):
                for k, part in enumerate(plane_modes(source[comp, i], y_last, z_last)):
                    planes[i, 4 * comp + k] = part
            return 0

        lax.fori_loop(0, count, body, 0)

    def shifted_operator(source, target, count, lead):
        to_modes(source, count + 2)

        def column(tile, _):
            y = pl.ds(pl.multiple_of(tile * 8, 8), 8)
            for half in range(NZ // 128):
                z = slice(128 * half, 128 * half + 128)
                low = [planes[0, k, y, z] for k in range(12)]
                held = None
                for i in range(count + 1):
                    high = [planes[i + 1, k, y, z] for k in range(12)]
                    e = weight[lead + i, y, z]
                    f = mode_forces(element_modes(low, high))
                    done = {}
                    f = {key: done.setdefault(id(val), val * e) for key, val in f.items()}
                    now = []
                    for comp in range(3):
                        for q in range(2):
                            for r in range(2):
                                k = 4 * comp + 2 * q + r
                                slope = f[comp, 1, q, r]
                                level = f.get((comp, 0, q, r))
                                below = -slope if level is None else level - slope
                                above = slope if level is None else level + slope
                                if held is not None:
                                    layers[i - 1, k, y, z] = held[k] + below
                                now.append(above)
                    held = now
                    low = high
            return 0

        lax.fori_loop(0, NY // 8, column, 0)

        def to_nodes(i, _):
            inv = inverse[lead + i]
            for comp in range(3):
                across = []
                for r in range(2):
                    level, slope = layers[i, 4 * comp + r], layers[i, 4 * comp + 2 + r]
                    across.append((level - slope) + prev_y(level + slope, y_first))
                level, slope = across
                force = (level - slope) + prev_z(level + slope, z_first)
                target[comp, i] = inv * force - source[comp, i + 1]
            return 0

        lax.fori_loop(0, count, to_nodes, 0)

    shifted_operator(w0, w1, 5, 1)
    shifted_operator(w1, basis.at[2], 3, 2)
    basis[0] = w0[:, 2:5]
    basis[1] = w1[:, 1:4]

    to_modes(basis.at[2], 3)

    def column(tile, summed):
        y = pl.ds(pl.multiple_of(tile * 8, 8), 8)
        for half in range(NZ // 128):
            z = slice(128 * half, 128 * half + 128)
            low = [planes[0, k, y, z] for k in range(12)]
            for i in range(2):
                high = [planes[i + 1, k, y, z] for k in range(12)]
                summed = summed + weight[3 + i, y, z] * mode_energy(element_modes(low, high))
                low = high
        return summed

    totals = [jnp.zeros((8, 128), jnp.float32) for _ in range(5)]
    totals.append(lax.fori_loop(0, NY // 8, column, jnp.zeros((8, 128), jnp.float32)))
    for i in range(2):
        m = mass[2 + i]
        for comp in range(3):
            v = [basis[k, comp, i] for k in range(3)]
            mv = [m * a for a in v]
            products = (mv[0] * v[0], mv[0] * v[1], mv[1] * v[1], mv[1] * v[2], mv[2] * v[2])
            for k, product in enumerate(products):
                part = product[:, :128] + product[:, 128:]
                totals[k] = totals[k] + ((part[0:8] + part[8:16]) + (part[16:24] + part[24:32]))
    sums = [jnp.sum(total, axis=0, keepdims=True) for total in totals]
    block = jnp.concatenate(sums + [jnp.zeros((2, 128), jnp.float32)], axis=0)
    for i in range(16):
        moments[i] = block


def step_sizes(nu):
    eta = [nu[k] + nu[k + 1] for k in range(4)] + [nu[5]]

    def form(v, values):
        summed = None
        for i in range(len(v)):
            for j in range(i, len(v)):
                term = (v[i] * v[j]) * values[i + j]
                term = term if i == j else 2.0 * term
                summed = term if summed is None else summed + term
        return summed

    first = nu[0] / eta[0]
    z = [1.0 - first, -first]
    now = form(z, nu)
    beta = now / nu[0]
    p = [z[0] + beta, z[1]]
    second = now / form(p, eta)
    last = [z[0] - second * p[0], z[1] - second * (p[0] + p[1]), -(second * p[1])]
    then = form(last, nu)
    beta = then / now
    q = [last[0] + beta * p[0], last[1] + beta * p[1], last[2]]
    third = then / form(q, eta)
    return [first + second * p[0] + third * q[0], second * p[1] + third * q[1], third * q[2]]


def combine_kernel(parts, basis, displacement, energies, planes, energy):
    y_first, y_last, z_first, z_last = plane_edges()
    total = parts[0]
    for i in range(1, 16):
        total = total + parts[i]
    nu = [jnp.sum(total[k : k + 1, :], axis=1, keepdims=True) for k in range(6)]
    coefficient = step_sizes(nu)
    wide = [jnp.broadcast_to(c, (NY, NZ)) for c in coefficient]
    for comp in range(3):
        for i in range(3):
            u = wide[0] * basis[0, comp, i] + wide[1] * basis[1, comp, i] + wide[2] * basis[2, comp, i]
            if i < 2:
                displacement[comp, i] = u
            for k, part in enumerate(plane_modes(u, y_last, z_last)):
                planes[i, 4 * comp + k] = part

    def column(tile, _):
        y = pl.ds(pl.multiple_of(tile * 8, 8), 8)
        for half in range(NZ // 128):
            z = slice(128 * half, 128 * half + 128)
            low = [planes[0, k, y, z] for k in range(12)]
            for i in range(2):
                high = [planes[i + 1, k, y, z] for k in range(12)]
                energy[i, y, z] = MODE_SCALE * mode_energy(element_modes(low, high))
                low = high
        return 0

    lax.fori_loop(0, NY // 8, column, 0)
    for load in range(LOADS):
        energies[load] = energy[:, 2 * load : 2 * load + 2, :]


def shards(density, fixed_mask, patch_index, patch_force):
    slab = lax.axis_index("space")
    vmem = pl.BlockSpec(memory_space=pltpu.VMEM)
    smem = pl.BlockSpec(memory_space=pltpu.SMEM)
    field = lambda *shape: pltpu.VMEM(shape + (NY, NZ), jnp.float32)
    planes = lambda *shape: jax.ShapeDtypeStruct(shape + (NY, NZ), jnp.float32)

    gathered = lax.all_to_all(jnp.broadcast_to(density[None], (LOADS,) + density.shape), "load", 0, 0, tiled=True)
    own, upper, lower, factor = pl.pallas_call(
        pack_kernel,
        out_shape=(planes(4), planes(1), planes(2), jax.ShapeDtypeStruct(density.shape, jnp.float32)),
        in_specs=[vmem] * 4,
        out_specs=(vmem,) * 4,
        scratch_shapes=[field(2)],
        compiler_params=pltpu.CompilerParams(vmem_limit_bytes=3 << 20),
        name="pack",
    )(gathered, density, fixed_mask, patch_index)
    shifted = lambda x, by: lax.ppermute(x, "space", [(i, (i + by) % 16) for i in range(16)])
    below, above, below_next, above_next = shifted(own, 1), shifted(own, -1), shifted(upper, 2), shifted(lower, -2)
    basis, moments = pl.pallas_call(
        krylov_kernel,
        out_shape=(planes(3, 3, 3), jax.ShapeDtypeStruct((16, 8, 128), jnp.float32)),
        in_specs=[smem, smem] + [vmem] * 5,
        out_specs=(vmem, vmem),
        scratch_shapes=[field(8), field(7), field(7), field(7), field(3, 7), field(3, 5), field(7, 12), field(5, 12)],
        compiler_params=pltpu.CompilerParams(vmem_limit_bytes=12 << 20),
        name="krylov",
    )(slab.astype(jnp.int32).reshape(1), patch_force[0], own, below, above, below_next, above_next)
    parts = lax.all_to_all(moments, "space", 0, 0, tiled=True)
    displacement, energies = pl.pallas_call(
        combine_kernel,
        out_shape=(
            planes(3, 2),
            jax.ShapeDtypeStruct((LOADS, 2, 2, NZ), jnp.float32),
        ),
        in_specs=[vmem, vmem],
        out_specs=(vmem, vmem),
        scratch_shapes=[field(3, 12), field(2)],
        compiler_params=pltpu.CompilerParams(vmem_limit_bytes=6 << 20),
        name="combine",
    )(parts, basis)
    received = lax.all_to_all(energies, "load", 0, 0, tiled=True)
    summed = jnp.sum(received, axis=0)
    sensitivity = factor * summed
    return (displacement[None], sensitivity)


def solution(mesh):
    in_specs = (
        P("space", "load", None),
        P("space", None, None),
        P("space", None, None),
        P("load", None, None),
    )
    out_specs = (P("load", None, "space", None, None), P("space", "load", None))
    return jax.shard_map(shards, mesh=mesh, in_specs=in_specs, out_specs=out_specs, check_vma=False)
```

```python
import jax
import jax.numpy as jnp
from jax import lax
from jax.experimental import pallas as pl
from jax.experimental.pallas import tpu as pltpu
from jax.sharding import PartitionSpec as P

NX, NY, NZ = 32, 32, 256
PATCHES = 16
LOADS = 16
void_stiffness = 0.001
poisson_ratio = 0.3
LAME = poisson_ratio / ((1.0 + poisson_ratio) * (1.0 - 2.0 * poisson_ratio))
SHEAR = 0.5 / (1.0 + poisson_ratio)
DIAGONAL = (LAME + 4.0 * SHEAR) / 9.0
MODE_SCALE = 1.0 / 16.0


def next_y(v, last):
    return jnp.where(last, 0.0, pltpu.roll(v, v.shape[0] - 1, 0))


def prev_y(v, first):
    return jnp.where(first, 0.0, pltpu.roll(v, 1, 0))


def next_z(v, last):
    return jnp.where(last, 0.0, pltpu.roll(v, v.shape[1] - 1, 1))


def prev_z(v, first):
    return jnp.where(first, 0.0, pltpu.roll(v, 1, 1))


def plane_edges():
    row = lax.broadcasted_iota(jnp.int32, (NY, NZ), 0)
    col = lax.broadcasted_iota(jnp.int32, (NY, NZ), 1)
    return row == 0, row == NY - 1, col == 0, col == NZ - 1


def plane_modes(v, y_last, z_last):
    ahead = next_z(v, z_last)
    out = []
    pair = (v + ahead, ahead - v)
    for part in pair:
        above = next_y(part, y_last)
        out.append((part + above, above - part))
    return [out[r][q] for q in range(2) for r in range(2)]


def element_modes(low, high):
    modes = {}
    for comp in range(3):
        for q in range(2):
            for r in range(2):
                a, b = low[4 * comp + 2 * q + r], high[4 * comp + 2 * q + r]
                if q + r > 0:
                    modes[comp, 0, q, r] = a + b
                modes[comp, 1, q, r] = b - a
    return modes


UNIT = ((1, 0, 0), (0, 1, 0), (0, 0, 1))
PAIRS = ((0, 1), (0, 2), (1, 2))


def both(i, j):
    return tuple(UNIT[i][k] + UNIT[j][k] for k in range(3))


BLOCKS = tuple(((i, both(i, j)), (k, both(k, j))) for j in range(3) for i, k in PAIRS if j not in (i, k))
TRIPLE = tuple((i, both(*[k for k in range(3) if k != i])) for i in range(3))


def mode_forces(h):
    out = {}
    trace = (h[(0,) + UNIT[0]] + h[(1,) + UNIT[1]] + h[(2,) + UNIT[2]]) * LAME
    for i in range(3):
        out[(i,) + UNIT[i]] = trace + (2.0 * SHEAR) * h[(i,) + UNIT[i]]
    for i, k in PAIRS:
        shear = SHEAR * (h[(i,) + UNIT[k]] + h[(k,) + UNIT[i]])
        out[(i,) + UNIT[k]] = shear
        out[(k,) + UNIT[i]] = shear
    for (i, a), (k, b) in BLOCKS:
        both_ = (LAME / 3.0) * (h[(i,) + a] + h[(k,) + b])
        out[(i,) + a] = both_ + SHEAR * h[(i,) + a]
        out[(k,) + b] = both_ + SHEAR * h[(k,) + b]
    total = h[(0,) + TRIPLE[0][1]] + h[(1,) + TRIPLE[1][1]] + h[(2,) + TRIPLE[2][1]]
    for i, a in TRIPLE:
        out[(i,) + a] = (SHEAR / 3.0) * (total + h[(i,) + a])
    for i in range(3):
        out[i, 1, 1, 1] = DIAGONAL * h[i, 1, 1, 1]
    return out


def mode_energy(h):
    trace = h[(0,) + UNIT[0]] + h[(1,) + UNIT[1]] + h[(2,) + UNIT[2]]
    summed = LAME * (trace * trace)
    normal = None
    for i in range(3):
        term = h[(i,) + UNIT[i]] * h[(i,) + UNIT[i]]
        normal = term if normal is None else normal + term
    summed = summed + (2.0 * SHEAR) * normal
    shear = None
    for i, k in PAIRS:
        pair = h[(i,) + UNIT[k]] + h[(k,) + UNIT[i]]
        term = pair * pair
        shear = term if shear is None else shear + term
    for (i, a), (k, b) in BLOCKS:
        shear = shear + (h[(i,) + a] * h[(i,) + a] + h[(k,) + b] * h[(k,) + b])
    blocks = None
    for (i, a), (k, b) in BLOCKS:
        pair = h[(i,) + a] + h[(k,) + b]
        term = pair * pair
        blocks = term if blocks is None else blocks + term
    summed = summed + SHEAR * shear + (LAME / 3.0) * blocks
    total = h[(0,) + TRIPLE[0][1]] + h[(1,) + TRIPLE[1][1]] + h[(2,) + TRIPLE[2][1]]
    triple = total * total
    corner = None
    for i, a in TRIPLE:
        triple = triple + h[(i,) + a] * h[(i,) + a]
        term = h[i, 1, 1, 1] * h[i, 1, 1, 1]
        corner = term if corner is None else corner + term
    return summed + (SHEAR / 3.0) * triple + DIAGONAL * corner


def code_of(fixed, patch):
    return jnp.where(fixed == 0, patch + 1, 0).astype(jnp.float32)


def pack_kernel(gathered, density, fixed, patches, own, upper, lower, factor, rows):
    for load in range(LOADS):
        rows[:, 2 * load : 2 * load + 2, :] = gathered[load]
    for i in range(2):
        rho = rows[i]
        layer = MODE_SCALE * (void_stiffness + (1.0 - void_stiffness) * (rho * rho * rho))
        code = code_of(fixed[i], patches[i])
        own[1 - i] = layer
        own[2 + i] = code
        if i == 0:
            lower[0] = layer
            lower[1] = code
        else:
            upper[0] = layer
    mine = density[...]
    factor[...] = (-3.0 * (1.0 - void_stiffness) / LOADS) * (mine * mine)


def krylov_kernel(place, table, own, below, above, below_next, above_next, basis, moments, *scratch):
    weight, codes, inverse, mass, w0, w1, planes, layers = scratch
    first = 2 * place[0] - 2
    y_first, y_last, z_first, z_last = plane_edges()

    layer_list = [(below_next, 0), (below, 1), (below, 0), (own, 1), (own, 0), (above, 1), (above, 0), (above_next, 0)]
    code_list = [(below, 2), (below, 3), (own, 2), (own, 3), (above, 2), (above, 3), (above_next, 1)]
    for target, offset, refs in ((weight, first - 1, layer_list), (codes, first, code_list)):
        for i, (ref, k) in enumerate(refs):
            inside = (offset + i >= 0) & (offset + i < NX)
            target[i] = ref[k] if ref is own else ref[k] * jnp.where(inside, 1.0, 0.0)

    def set_plane(i, _):
        code = codes[i]
        both_layers = weight[i] + weight[i + 1]
        across = both_layers + prev_y(both_layers, y_first)
        diag = (DIAGONAL / MODE_SCALE) * (across + prev_z(across, z_first))
        inv = jnp.where(code > 0.5, 1.0 / diag, 0.0)
        inverse[i] = inv
        mass[i] = diag
        scaled = inv * (1.0 + 2.0 * (first + i).astype(jnp.float32) / (NX - 1))
        patch = code.astype(jnp.int32)
        for comp in range(3):
            row = jnp.broadcast_to(table[comp : comp + 1, :], (8, 128))
            for y in range(0, NY, 8):
                for z in range(0, NZ, 128):
                    force = jnp.take_along_axis(row, patch[y : y + 8, z : z + 128], axis=1)
                    w0[comp, i, y : y + 8, z : z + 128] = scaled[y : y + 8, z : z + 128] * force
        return 0

    lax.fori_loop(0, 7, set_plane, 0, unroll=True)

    def to_modes(source, count):
        def body(i, _):
            for comp in range(3):
                for k, part in enumerate(plane_modes(source[comp, i], y_last, z_last)):
                    planes[i, 4 * comp + k] = part
            return 0

        lax.fori_loop(0, count, body, 0, unroll=True)

    def shifted_operator(source, target, count, lead):
        to_modes(source, count + 2)

        def column(tile, _):
            y = pl.ds(pl.multiple_of(tile * 8, 8), 8)
            for half in range(NZ // 128):
                z = slice(128 * half, 128 * half + 128)
                low = [planes[0, k, y, z] for k in range(12)]
                held = None
                for i in range(count + 1):
                    high = [planes[i + 1, k, y, z] for k in range(12)]
                    e = weight[lead + i, y, z]
                    f = mode_forces(element_modes(low, high))
                    done = {}
                    f = {key: done.setdefault(id(val), val * e) for key, val in f.items()}
                    now = []
                    for comp in range(3):
                        for q in range(2):
                            for r in range(2):
                                k = 4 * comp + 2 * q + r
                                slope = f[comp, 1, q, r]
                                level = f.get((comp, 0, q, r))
                                below = -slope if level is None else level - slope
                                above = slope if level is None else level + slope
                                if held is not None:
                                    layers[i - 1, k, y, z] = held[k] + below
                                now.append(above)
                    held = now
                    low = high
            return 0

        lax.fori_loop(0, NY // 8, column, 0, unroll=True)

        def to_nodes(i, _):
            inv = inverse[lead + i]
            for comp in range(3):
                across = []
                for r in range(2):
                    level, slope = layers[i, 4 * comp + r], layers[i, 4 * comp + 2 + r]
                    across.append((level - slope) + prev_y(level + slope, y_first))
                level, slope = across
                force = (level - slope) + prev_z(level + slope, z_first)
                target[comp, i] = inv * force - source[comp, i + 1]
            return 0

        lax.fori_loop(0, count, to_nodes, 0, unroll=True)

    shifted_operator(w0, w1, 5, 1)
    shifted_operator(w1, basis.at[2], 3, 2)
    basis[0] = w0[:, 2:5]
    basis[1] = w1[:, 1:4]

    to_modes(basis.at[2], 3)

    def column(tile, summed):
        y = pl.ds(pl.multiple_of(tile * 8, 8), 8)
        for half in range(NZ // 128):
            z = slice(128 * half, 128 * half + 128)
            low = [planes[0, k, y, z] for k in range(12)]
            for i in range(2):
                high = [planes[i + 1, k, y, z] for k in range(12)]
                summed = summed + weight[3 + i, y, z] * mode_energy(element_modes(low, high))
                low = high
        return summed

    totals = [jnp.zeros((8, 128), jnp.float32) for _ in range(5)]
    totals.append(lax.fori_loop(0, NY // 8, column, jnp.zeros((8, 128), jnp.float32), unroll=True))
    for i in range(2):
        m = mass[2 + i]
        for comp in range(3):
            v = [basis[k, comp, i] for k in range(3)]
            mv = [m * a for a in v]
            products = (mv[0] * v[0], mv[0] * v[1], mv[1] * v[1], mv[1] * v[2], mv[2] * v[2])
            for k, product in enumerate(products):
                part = product[:, :128] + product[:, 128:]
                totals[k] = totals[k] + ((part[0:8] + part[8:16]) + (part[16:24] + part[24:32]))
    sums = [jnp.sum(total, axis=0, keepdims=True) for total in totals]
    block = jnp.concatenate(sums + [jnp.zeros((2, 128), jnp.float32)], axis=0)
    for i in range(16):
        moments[i] = block


def step_sizes(nu):
    eta = [nu[k] + nu[k + 1] for k in range(4)] + [nu[5]]

    def form(v, values):
        summed = None
        for i in range(len(v)):
            for j in range(i, len(v)):
                term = (v[i] * v[j]) * values[i + j]
                term = term if i == j else 2.0 * term
                summed = term if summed is None else summed + term
        return summed

    first = nu[0] / eta[0]
    z = [1.0 - first, -first]
    now = form(z, nu)
    beta = now / nu[0]
    p = [z[0] + beta, z[1]]
    second = now / form(p, eta)
    last = [z[0] - second * p[0], z[1] - second * (p[0] + p[1]), -(second * p[1])]
    then = form(last, nu)
    beta = then / now
    q = [last[0] + beta * p[0], last[1] + beta * p[1], last[2]]
    third = then / form(q, eta)
    return [first + second * p[0] + third * q[0], second * p[1] + third * q[1], third * q[2]]


def combine_kernel(parts, basis, displacement, energies, planes, energy):
    y_first, y_last, z_first, z_last = plane_edges()
    total = parts[0]
    for i in range(1, 16):
        total = total + parts[i]
    nu = [jnp.sum(total[k : k + 1, :], axis=1, keepdims=True) for k in range(6)]
    coefficient = step_sizes(nu)
    wide = [jnp.broadcast_to(c, (NY, NZ)) for c in coefficient]
    for comp in range(3):
        for i in range(3):
            u = wide[0] * basis[0, comp, i] + wide[1] * basis[1, comp, i] + wide[2] * basis[2, comp, i]
            if i < 2:
                displacement[comp, i] = u
            for k, part in enumerate(plane_modes(u, y_last, z_last)):
                planes[i, 4 * comp + k] = part

    def column(tile, _):
        y = pl.ds(pl.multiple_of(tile * 8, 8), 8)
        for half in range(NZ // 128):
            z = slice(128 * half, 128 * half + 128)
            low = [planes[0, k, y, z] for k in range(12)]
            for i in range(2):
                high = [planes[i + 1, k, y, z] for k in range(12)]
                energy[i, y, z] = MODE_SCALE * mode_energy(element_modes(low, high))
                low = high
        return 0

    lax.fori_loop(0, NY // 8, column, 0, unroll=True)
    for load in range(LOADS):
        energies[load] = energy[:, 2 * load : 2 * load + 2, :]


def shards(density, fixed_mask, patch_index, patch_force):
    slab = lax.axis_index("space")
    vmem = pl.BlockSpec(memory_space=pltpu.VMEM)
    smem = pl.BlockSpec(memory_space=pltpu.SMEM)
    field = lambda *shape: pltpu.VMEM(shape + (NY, NZ), jnp.float32)
    planes = lambda *shape: jax.ShapeDtypeStruct(shape + (NY, NZ), jnp.float32)

    gathered = lax.all_to_all(jnp.broadcast_to(density[None], (LOADS,) + density.shape), "load", 0, 0, tiled=True)
    own, upper, lower, factor = pl.pallas_call(
        pack_kernel,
        out_shape=(planes(4), planes(1), planes(2), jax.ShapeDtypeStruct(density.shape, jnp.float32)),
        in_specs=[vmem] * 4,
        out_specs=(vmem,) * 4,
        scratch_shapes=[field(2)],
        compiler_params=pltpu.CompilerParams(vmem_limit_bytes=3 << 20),
        name="pack",
    )(gathered, density, fixed_mask, patch_index)
    shifted = lambda x, by: lax.ppermute(x, "space", [(i, (i + by) % 16) for i in range(16)])
    below, above, below_next, above_next = shifted(own, 1), shifted(own, -1), shifted(upper, 2), shifted(lower, -2)
    table = jnp.pad(patch_force[0], ((0, 5), (1, 127 - PATCHES)))
    basis, moments = pl.pallas_call(
        krylov_kernel,
        out_shape=(planes(3, 3, 3), jax.ShapeDtypeStruct((16, 8, 128), jnp.float32)),
        in_specs=[smem] + [vmem] * 6,
        out_specs=(vmem, vmem),
        scratch_shapes=[field(8), field(7), field(7), field(7), field(3, 7), field(3, 5), field(7, 12), field(5, 12)],
        compiler_params=pltpu.CompilerParams(vmem_limit_bytes=12 << 20),
        name="krylov",
    )(slab.astype(jnp.int32).reshape(1), table, own, below, above, below_next, above_next)
    parts = lax.all_to_all(moments, "space", 0, 0, tiled=True)
    displacement, energies = pl.pallas_call(
        combine_kernel,
        out_shape=(
            planes(3, 2),
            jax.ShapeDtypeStruct((LOADS, 2, 2, NZ), jnp.float32),
        ),
        in_specs=[vmem, vmem],
        out_specs=(vmem, vmem),
        scratch_shapes=[field(3, 12), field(2)],
        compiler_params=pltpu.CompilerParams(vmem_limit_bytes=6 << 20),
        name="combine",
    )(parts, basis)
    received = lax.all_to_all(energies, "load", 0, 0, tiled=True)
    summed = jnp.sum(received, axis=0)
    sensitivity = factor * summed
    return (displacement[None], sensitivity)


def solution(mesh):
    in_specs = (
        P("space", "load", None),
        P("space", None, None),
        P("space", None, None),
        P("load", None, None),
    )
    out_specs = (P("load", None, "space", None, None), P("space", "load", None))
    return jax.shard_map(shards, mesh=mesh, in_specs=in_specs, out_specs=out_specs, check_vma=False)
```

```python
import jax
import jax.numpy as jnp
from jax import lax
from jax.experimental import pallas as pl
from jax.experimental.pallas import tpu as pltpu
from jax.sharding import PartitionSpec as P

NX, NY, NZ = 32, 32, 256
PATCHES = 16
LOADS = 16
void_stiffness = 0.001
poisson_ratio = 0.3
LAME = poisson_ratio / ((1.0 + poisson_ratio) * (1.0 - 2.0 * poisson_ratio))
SHEAR = 0.5 / (1.0 + poisson_ratio)
DIAGONAL = (LAME + 4.0 * SHEAR) / 9.0
MODE_SCALE = 1.0 / 16.0


def next_y(v, last):
    return jnp.where(last, 0.0, pltpu.roll(v, v.shape[0] - 1, 0))


def prev_y(v, first):
    return jnp.where(first, 0.0, pltpu.roll(v, 1, 0))


def next_z(v, last):
    return jnp.where(last, 0.0, pltpu.roll(v, v.shape[1] - 1, 1))


def prev_z(v, first):
    return jnp.where(first, 0.0, pltpu.roll(v, 1, 1))


def plane_edges():
    row = lax.broadcasted_iota(jnp.int32, (NY, NZ), 0)
    col = lax.broadcasted_iota(jnp.int32, (NY, NZ), 1)
    return row == 0, row == NY - 1, col == 0, col == NZ - 1


def plane_modes(v, y_last, z_last):
    ahead = next_z(v, z_last)
    out = []
    pair = (v + ahead, ahead - v)
    for part in pair:
        above = next_y(part, y_last)
        out.append((part + above, above - part))
    return [out[r][q] for q in range(2) for r in range(2)]


def element_modes(low, high):
    modes = {}
    for comp in range(3):
        for q in range(2):
            for r in range(2):
                a, b = low[4 * comp + 2 * q + r], high[4 * comp + 2 * q + r]
                if q + r > 0:
                    modes[comp, 0, q, r] = a + b
                modes[comp, 1, q, r] = b - a
    return modes


UNIT = ((1, 0, 0), (0, 1, 0), (0, 0, 1))
PAIRS = ((0, 1), (0, 2), (1, 2))


def both(i, j):
    return tuple(UNIT[i][k] + UNIT[j][k] for k in range(3))


BLOCKS = tuple(((i, both(i, j)), (k, both(k, j))) for j in range(3) for i, k in PAIRS if j not in (i, k))
TRIPLE = tuple((i, both(*[k for k in range(3) if k != i])) for i in range(3))


def mode_forces(h):
    out = {}
    trace = (h[(0,) + UNIT[0]] + h[(1,) + UNIT[1]] + h[(2,) + UNIT[2]]) * LAME
    for i in range(3):
        out[(i,) + UNIT[i]] = trace + (2.0 * SHEAR) * h[(i,) + UNIT[i]]
    for i, k in PAIRS:
        shear = SHEAR * (h[(i,) + UNIT[k]] + h[(k,) + UNIT[i]])
        out[(i,) + UNIT[k]] = shear
        out[(k,) + UNIT[i]] = shear
    for (i, a), (k, b) in BLOCKS:
        both_ = (LAME / 3.0) * (h[(i,) + a] + h[(k,) + b])
        out[(i,) + a] = both_ + SHEAR * h[(i,) + a]
        out[(k,) + b] = both_ + SHEAR * h[(k,) + b]
    total = h[(0,) + TRIPLE[0][1]] + h[(1,) + TRIPLE[1][1]] + h[(2,) + TRIPLE[2][1]]
    for i, a in TRIPLE:
        out[(i,) + a] = (SHEAR / 3.0) * (total + h[(i,) + a])
    for i in range(3):
        out[i, 1, 1, 1] = DIAGONAL * h[i, 1, 1, 1]
    return out


def mode_energy(h):
    trace = h[(0,) + UNIT[0]] + h[(1,) + UNIT[1]] + h[(2,) + UNIT[2]]
    summed = LAME * (trace * trace)
    normal = None
    for i in range(3):
        term = h[(i,) + UNIT[i]] * h[(i,) + UNIT[i]]
        normal = term if normal is None else normal + term
    summed = summed + (2.0 * SHEAR) * normal
    shear = None
    for i, k in PAIRS:
        pair = h[(i,) + UNIT[k]] + h[(k,) + UNIT[i]]
        term = pair * pair
        shear = term if shear is None else shear + term
    for (i, a), (k, b) in BLOCKS:
        shear = shear + (h[(i,) + a] * h[(i,) + a] + h[(k,) + b] * h[(k,) + b])
    blocks = None
    for (i, a), (k, b) in BLOCKS:
        pair = h[(i,) + a] + h[(k,) + b]
        term = pair * pair
        blocks = term if blocks is None else blocks + term
    summed = summed + SHEAR * shear + (LAME / 3.0) * blocks
    total = h[(0,) + TRIPLE[0][1]] + h[(1,) + TRIPLE[1][1]] + h[(2,) + TRIPLE[2][1]]
    triple = total * total
    corner = None
    for i, a in TRIPLE:
        triple = triple + h[(i,) + a] * h[(i,) + a]
        term = h[i, 1, 1, 1] * h[i, 1, 1, 1]
        corner = term if corner is None else corner + term
    return summed + (SHEAR / 3.0) * triple + DIAGONAL * corner


def code_of(fixed, patch):
    return jnp.where(fixed == 0, patch + 1, 0).astype(jnp.float32)


def pack_kernel(gathered, density, fixed, patches, own, upper, lower, factor, rows):
    for load in range(LOADS):
        rows[:, 2 * load : 2 * load + 2, :] = gathered[load]
    for i in range(2):
        rho = rows[i]
        layer = MODE_SCALE * (void_stiffness + (1.0 - void_stiffness) * (rho * rho * rho))
        code = code_of(fixed[i], patches[i])
        own[1 - i] = layer
        own[2 + i] = code
        if i == 0:
            lower[0] = layer
            lower[1] = code
        else:
            upper[0] = layer
    mine = density[...]
    factor[...] = (-3.0 * (1.0 - void_stiffness) / LOADS) * (mine * mine)


def krylov_kernel(place, table, own, below, above, below_next, above_next, basis, moments, *scratch):
    weight, codes, inverse, mass, w0, w1, planes, layers = scratch
    first = 2 * place[0] - 2
    y_first, y_last, z_first, z_last = plane_edges()

    layer_list = [(below_next, 0), (below, 1), (below, 0), (own, 1), (own, 0), (above, 1), (above, 0), (above_next, 0)]
    code_list = [(below, 2), (below, 3), (own, 2), (own, 3), (above, 2), (above, 3), (above_next, 1)]
    for target, offset, refs in ((weight, first - 1, layer_list), (codes, first, code_list)):
        for i, (ref, k) in enumerate(refs):
            inside = (offset + i >= 0) & (offset + i < NX)
            target[i] = ref[k] if ref is own else ref[k] * jnp.where(inside, 1.0, 0.0)

    def set_plane(i, _):
        code = codes[i]
        both_layers = weight[i] + weight[i + 1]
        across = both_layers + prev_y(both_layers, y_first)
        diag = (DIAGONAL / MODE_SCALE) * (across + prev_z(across, z_first))
        inv = jnp.where(code > 0.5, 1.0 / diag, 0.0)
        inverse[i] = inv
        mass[i] = diag
        scaled = inv * (1.0 + 2.0 * (first + i).astype(jnp.float32) / (NX - 1))
        patch = code.astype(jnp.int32)
        for comp in range(3):
            row = jnp.broadcast_to(table[comp : comp + 1, :], (8, 128))
            for y in range(0, NY, 8):
                for z in range(0, NZ, 128):
                    force = jnp.take_along_axis(row, patch[y : y + 8, z : z + 128], axis=1)
                    w0[comp, i, y : y + 8, z : z + 128] = scaled[y : y + 8, z : z + 128] * force
        return 0

    lax.fori_loop(0, 7, set_plane, 0, unroll=True)

    def to_modes(source, count):
        def body(i, _):
            for comp in range(3):
                for k, part in enumerate(plane_modes(source[comp, i], y_last, z_last)):
                    planes[i, 4 * comp + k] = part
            return 0

        lax.fori_loop(0, count, body, 0, unroll=True)

    def shifted_operator(source, target, count, lead):
        to_modes(source, count + 2)

        def column(tile, _):
            y = pl.ds(pl.multiple_of(tile * 8, 8), 8)
            for half in range(NZ // 128):
                z = slice(128 * half, 128 * half + 128)
                low = [planes[0, k, y, z] for k in range(12)]
                held = None
                for i in range(count + 1):
                    high = [planes[i + 1, k, y, z] for k in range(12)]
                    e = weight[lead + i, y, z]
                    f = mode_forces(element_modes(low, high))
                    done = {}
                    f = {key: done.setdefault(id(val), val * e) for key, val in f.items()}
                    now = []
                    for comp in range(3):
                        for q in range(2):
                            for r in range(2):
                                k = 4 * comp + 2 * q + r
                                slope = f[comp, 1, q, r]
                                level = f.get((comp, 0, q, r))
                                below = -slope if level is None else level - slope
                                above = slope if level is None else level + slope
                                if held is not None:
                                    layers[i - 1, k, y, z] = held[k] + below
                                now.append(above)
                    held = now
                    low = high
            return 0

        lax.fori_loop(0, NY // 8, column, 0, unroll=True)

        def to_nodes(i, _):
            inv = inverse[lead + i]
            for comp in range(3):
                across = []
                for r in range(2):
                    level, slope = layers[i, 4 * comp + r], layers[i, 4 * comp + 2 + r]
                    across.append((level - slope) + prev_y(level + slope, y_first))
                level, slope = across
                force = (level - slope) + prev_z(level + slope, z_first)
                target[comp, i] = inv * force - source[comp, i + 1]
            return 0

        lax.fori_loop(0, count, to_nodes, 0, unroll=True)

    shifted_operator(w0, w1, 5, 1)
    shifted_operator(w1, basis.at[2], 3, 2)
    basis[0] = w0[:, 2:5]
    basis[1] = w1[:, 1:4]

    to_modes(basis.at[2], 3)

    def column(tile, summed):
        y = pl.ds(pl.multiple_of(tile * 8, 8), 8)
        for half in range(NZ // 128):
            z = slice(128 * half, 128 * half + 128)
            low = [planes[0, k, y, z] for k in range(12)]
            for i in range(2):
                high = [planes[i + 1, k, y, z] for k in range(12)]
                summed = summed + weight[3 + i, y, z] * mode_energy(element_modes(low, high))
                low = high
        return summed

    totals = [jnp.zeros((8, 128), jnp.float32) for _ in range(5)]
    totals.append(lax.fori_loop(0, NY // 8, column, jnp.zeros((8, 128), jnp.float32), unroll=True))
    for i in range(2):
        m = mass[2 + i]
        for comp in range(3):
            v = [basis[k, comp, i] for k in range(3)]
            mv = [m * a for a in v]
            products = (mv[0] * v[0], mv[0] * v[1], mv[1] * v[1], mv[1] * v[2], mv[2] * v[2])
            for k, product in enumerate(products):
                part = product[:, :128] + product[:, 128:]
                totals[k] = totals[k] + ((part[0:8] + part[8:16]) + (part[16:24] + part[24:32]))
    sums = [jnp.sum(total, axis=0, keepdims=True) for total in totals]
    block = jnp.concatenate(sums + [jnp.zeros((2, 128), jnp.float32)], axis=0)
    for i in range(16):
        moments[i] = block


def step_sizes(nu):
    eta = [nu[k] + nu[k + 1] for k in range(4)] + [nu[5]]

    def form(v, values):
        summed = None
        for i in range(len(v)):
            for j in range(i, len(v)):
                term = (v[i] * v[j]) * values[i + j]
                term = term if i == j else 2.0 * term
                summed = term if summed is None else summed + term
        return summed

    def ratio(top, bottom):
        return jnp.where((top > 0.0) & (bottom > 0.0), top / bottom, 0.0)

    first = nu[0] / eta[0]
    z = [1.0 - first, -first]
    now = form(z, nu)
    beta = now / nu[0]
    p = [z[0] + beta, z[1]]
    second = ratio(now, form(p, eta))
    last = [z[0] - second * p[0], z[1] - second * (p[0] + p[1]), -(second * p[1])]
    then = jnp.where(second > 0.0, form(last, nu), 0.0)
    beta = ratio(then, now)
    q = [last[0] + beta * p[0], last[1] + beta * p[1], last[2]]
    third = ratio(then, form(q, eta))
    return [first + second * p[0] + third * q[0], second * p[1] + third * q[1], third * q[2]]


def combine_kernel(parts, basis, displacement, energies, planes, energy):
    y_first, y_last, z_first, z_last = plane_edges()
    total = parts[0]
    for i in range(1, 16):
        total = total + parts[i]
    nu = [jnp.sum(total[k : k + 1, :], axis=1, keepdims=True) for k in range(6)]
    coefficient = step_sizes(nu)
    wide = [jnp.broadcast_to(c, (NY, NZ)) for c in coefficient]
    for comp in range(3):
        for i in range(3):
            u = wide[0] * basis[0, comp, i] + wide[1] * basis[1, comp, i] + wide[2] * basis[2, comp, i]
            if i < 2:
                displacement[comp, i] = u
            for k, part in enumerate(plane_modes(u, y_last, z_last)):
                planes[i, 4 * comp + k] = part

    def column(tile, _):
        y = pl.ds(pl.multiple_of(tile * 8, 8), 8)
        for half in range(NZ // 128):
            z = slice(128 * half, 128 * half + 128)
            low = [planes[0, k, y, z] for k in range(12)]
            for i in range(2):
                high = [planes[i + 1, k, y, z] for k in range(12)]
                energy[i, y, z] = MODE_SCALE * mode_energy(element_modes(low, high))
                low = high
        return 0

    lax.fori_loop(0, NY // 8, column, 0, unroll=True)
    for load in range(LOADS):
        energies[load] = energy[:, 2 * load : 2 * load + 2, :]


def shards(density, fixed_mask, patch_index, patch_force):
    slab = lax.axis_index("space")
    vmem = pl.BlockSpec(memory_space=pltpu.VMEM)
    smem = pl.BlockSpec(memory_space=pltpu.SMEM)
    field = lambda *shape: pltpu.VMEM(shape + (NY, NZ), jnp.float32)
    planes = lambda *shape: jax.ShapeDtypeStruct(shape + (NY, NZ), jnp.float32)

    gathered = lax.all_to_all(jnp.broadcast_to(density[None], (LOADS,) + density.shape), "load", 0, 0, tiled=True)
    own, upper, lower, factor = pl.pallas_call(
        pack_kernel,
        out_shape=(planes(4), planes(1), planes(2), jax.ShapeDtypeStruct(density.shape, jnp.float32)),
        in_specs=[vmem] * 4,
        out_specs=(vmem,) * 4,
        scratch_shapes=[field(2)],
        compiler_params=pltpu.CompilerParams(vmem_limit_bytes=3 << 20),
        name="pack",
    )(gathered, density, fixed_mask, patch_index)
    shifted = lambda x, by: lax.ppermute(x, "space", [(i, (i + by) % 16) for i in range(16)])
    below, above, below_next, above_next = shifted(own, 1), shifted(own, -1), shifted(upper, 2), shifted(lower, -2)
    table = jnp.pad(patch_force[0], ((0, 5), (1, 127 - PATCHES)))
    basis, moments = pl.pallas_call(
        krylov_kernel,
        out_shape=(planes(3, 3, 3), jax.ShapeDtypeStruct((16, 8, 128), jnp.float32)),
        in_specs=[smem] + [vmem] * 6,
        out_specs=(vmem, vmem),
        scratch_shapes=[field(8), field(7), field(7), field(7), field(3, 7), field(3, 5), field(7, 12), field(5, 12)],
        compiler_params=pltpu.CompilerParams(vmem_limit_bytes=12 << 20),
        name="krylov",
    )(slab.astype(jnp.int32).reshape(1), table, own, below, above, below_next, above_next)
    parts = lax.all_to_all(moments, "space", 0, 0, tiled=True)
    displacement, energies = pl.pallas_call(
        combine_kernel,
        out_shape=(
            planes(3, 2),
            jax.ShapeDtypeStruct((LOADS, 2, 2, NZ), jnp.float32),
        ),
        in_specs=[vmem, vmem],
        out_specs=(vmem, vmem),
        scratch_shapes=[field(3, 12), field(2)],
        compiler_params=pltpu.CompilerParams(vmem_limit_bytes=6 << 20),
        name="combine",
    )(parts, basis)
    received = lax.all_to_all(energies, "load", 0, 0, tiled=True)
    summed = jnp.sum(received, axis=0)
    sensitivity = factor * summed
    return (displacement[None], sensitivity)


def solution(mesh):
    in_specs = (
        P("space", "load", None),
        P("space", None, None),
        P("space", None, None),
        P("load", None, None),
    )
    out_specs = (P("load", None, "space", None, None), P("space", "load", None))
    return jax.shard_map(shards, mesh=mesh, in_specs=in_specs, out_specs=out_specs, check_vma=False)
```
